32 devices in a mesh: gx: 4 (over z), gy: 8 (over y, x, core).
Axes of the slice: x: 2, y: 2, z: 4, core: 2. Of those that a mesh axis runs over, the one named last changes fastest.
Arguments:
- populations: float32 [27, 16, 128, 128], P(None, 'gx', 'gy'), may hold values from 0.01 to 0.07
- species: float32 [7, 20, 16, 128, 128], P(None, None, 'gx', 'gy'), may hold values from 0 to 0.4
- node_type: int32 [16, 128, 128], P('gx', 'gy'), may hold values from 0 to 3, as said below
- reactions: int32 [84, 3], replicated, may hold values from 0 to 19
- rate_const: float32 [84], replicated, may hold values from 0.005 to 0.05
- species_rate: float32 [20], replicated, may hold values from 0.7 to 1.8
- inlet_mix: float32 [2, 20], replicated, may hold values from 0 to 2
Outputs:
- new_populations: float32 [27, 16, 128, 128], P(None, 'gx', 'gy')
- new_species: float32 [7, 20, 16, 128, 128], P(None, None, 'gx', 'gy')
The draws below stay inside these ranges and needn't reach their ends.
Inputs may be any that keep to these rules, and one draw needn't show every extreme that they name: `node_type`: rows y = 0 and y = 127 hold only walls and inlets: fuel inlets (2) in row 0 and oxidizer inlets (3) in row 127, for third coordinates from 32 to 95, walls elsewhere in these rows; other rows hold fluid (0) and scattered walls (1).
All inputs are finite; a program needn't handle non-finite values.
Results may differ from the reference program's by a relative error of at most 0.0001.
Values sent between devices are 32-bit elements; how exact they have to be, the bound alone decides.
No kernel may reach another device: no remote copies, remote signals or barrier semaphores. Data moves between devices by JAX's collectives and lax.ppermute only.
A program may use at most 128 MiB of HBM per device.

```python
import math
import jax
import jax.numpy as jnp
from jax import lax

NZ = 128
NS = 20
NR = 84
SUBSTEPS = 3
NX = 16
NY = 128


def draw_node_type(key, part):
    obstacle_draw = jax.random.randint(jax.random.fold_in(key, 7), (NX, NY, NZ), 0, 40)
    node_kinds = jnp.where(obstacle_draw == 0, 1, 0)
    row_index = lax.broadcasted_iota(jnp.int32, (NX, NY, NZ), 1)
    depth_index = lax.broadcasted_iota(jnp.int32, (NX, NY, NZ), 2)
    in_middle = (depth_index >= NZ // 4) & (depth_index < 3 * NZ // 4)
    node_kinds = jnp.where(row_index == 0, jnp.where(in_middle, 2, 1), node_kinds)
    node_kinds = jnp.where(row_index == NY - 1, jnp.where(in_middle, 3, 1), node_kinds)
    return node_kinds.astype(jnp.int32)


def set_ends(entries, rng, low, largest):
    longest = entries.shape.index(max(entries.shape))
    spots = []
    for shift in (0, 1):
        where = [jax.random.randint(jax.random.fold_in(rng, axis), (), 0, length) for axis, length in enumerate(entries.shape)]
        where[longest] = (where[longest] + shift) % entries.shape[longest]
        spots.append(tuple(where))
    return entries.at[spots[0]].set(low).at[spots[1]].set(largest)


def shard_levels(own_key, dims, pieces, low, high):
    level = 1.0
    for axis_at, shards_of in pieces:
        draws = jax.random.uniform(jax.random.fold_in(jax.random.fold_in(own_key, 6), axis_at), (shards_of,), jnp.float32, low / len(pieces), high / len(pieces))
        level = level * jnp.repeat(jnp.exp(draws), dims[axis_at] // shards_of).reshape((-1,) + (1,) * (len(dims) - 1 - axis_at))
    return level


def setup_inputs(seed: int = 0) -> dict:
    key_of = jax.random.split(jax.random.key(seed), 8)
    return {
        "populations": jnp.clip(0.01 + 0.060000001 * jax.random.uniform(key_of[0], (27, NX, NY, NZ), jnp.float32) ** shard_levels(key_of[0], (27, NX, NY, NZ), ((1, 4), (2, 8)), -0.2, 0.2), 0.01, 0.07),
        "species": jnp.clip(0.4 * jax.random.uniform(key_of[1], (7, NS, NX, NY, NZ), jnp.float32) ** shard_levels(key_of[1], (7, NS, NX, NY, NZ), ((2, 4), (3, 8)), -0.2, 0.2), 0.0, 0.4),
        "node_type": draw_node_type(jax.random.fold_in(key_of[7], 71), 0),
        "reactions": set_ends(jax.random.randint(key_of[3], (NR, 3), 0, NS), jax.random.fold_in(key_of[3], 1), 0, NS - 1).astype(jnp.int32),
        "rate_const": jnp.clip(jnp.exp(jax.random.uniform(key_of[4], (NR,), jnp.float32, math.log(0.005), math.log(0.05))), 0.005, 0.05),
        "species_rate": jnp.clip(jnp.exp(jax.random.uniform(key_of[5], (NS,), jnp.float32, math.log(0.7), math.log(1.8))), 0.7, 1.8),
        "inlet_mix": jnp.clip(jax.random.uniform(key_of[6], (2, NS), jnp.float32, 0.0, 2.0), 0.0, 2.0),
    }


flow_rate = 1.6
inlet_speed = 0.05


def flow_tables():
    velocities = [(first, second, third) for first in (-1, 0, 1) for second in (-1, 0, 1) for third in (-1, 0, 1)]
    table = [8.0 / 27, 2.0 / 27, 1.0 / 54, 1.0 / 216]
    weights = [table[abs(first) + abs(second) + abs(third)] for first, second, third in velocities]
    return velocities, weights, list(range(26, -1, -1))


def species_tables():
    velocities = [(0, 0, 0), (1, 0, 0), (-1, 0, 0), (0, 1, 0), (0, -1, 0), (0, 0, 1), (0, 0, -1)]
    weights = [0.25, 0.125, 0.125, 0.125, 0.125, 0.125, 0.125]
    return velocities, weights, [0, 2, 1, 4, 3, 6, 5]


def component(velocities, which):
    return [float(entry[which]) for entry in velocities]


def column(values, extra):
    return jnp.asarray(values, jnp.float32).reshape((-1,) + (1,) * extra)


def equilibrium(density, flow_x, flow_y, flow_z, velocities, weights):
    along = (column(component(velocities, 0), 3) * flow_x + column(component(velocities, 1), 3) * flow_y
             + column(component(velocities, 2), 3) * flow_z)
    speed_sq = flow_x * flow_x + flow_y * flow_y + flow_z * flow_z
    return column(weights, 3) * density * (1.0 + 3.0 * along + 4.5 * along * along - 1.5 * speed_sq)


def stream(field, velocities):
    step_x = column(component(velocities, 0), 3)
    step_y = column(component(velocities, 1), 3)
    step_z = column(component(velocities, 2), 3)
    field = jnp.where(step_x > 0, jnp.roll(field, 1, 1), jnp.where(step_x < 0, jnp.roll(field, -1, 1), field))
    zero_row = jnp.zeros_like(field[:, :, :1])
    shifted_up = jnp.concatenate([zero_row, field[:, :, :-1]], 2)
    shifted_down = jnp.concatenate([field[:, :, 1:], zero_row], 2)
    field = jnp.where(step_y > 0, shifted_up, jnp.where(step_y < 0, shifted_down, field))
    return jnp.where(step_z > 0, jnp.roll(field, 1, 3), jnp.where(step_z < 0, jnp.roll(field, -1, 3), field))


def reference(populations, species, node_type, reactions, rate_const, species_rate, inlet_mix):
    high = lax.Precision.HIGHEST
    velocities, weights, reverse = flow_tables()
    density = jnp.sum(populations, 0)
    flow_x = jnp.tensordot(column(component(velocities, 0), 0), populations, axes=(0, 0), precision=high) / density
    flow_y = jnp.tensordot(column(component(velocities, 1), 0), populations, axes=(0, 0), precision=high) / density
    flow_z = jnp.tensordot(column(component(velocities, 2), 0), populations, axes=(0, 0), precision=high) / density
    post = populations + flow_rate * (equilibrium(density, flow_x, flow_y, flow_z, velocities, weights) - populations)
    moved = stream(post, velocities)
    is_wall = (node_type == 1)[None]
    at_fuel = (node_type == 2)[None]
    at_oxidizer = (node_type == 3)[None]
    unit = jnp.float32(1.0)
    still = jnp.float32(0.0)
    fuel_state = equilibrium(unit, still, jnp.float32(inlet_speed), still, velocities, weights)
    oxidizer_state = equilibrium(unit, still, jnp.float32(-inlet_speed), still, velocities, weights)
    new_populations = jnp.where(is_wall, moved[jnp.asarray(reverse, jnp.int32)], moved)
    new_populations = jnp.where(at_fuel, fuel_state, new_populations)
    new_populations = jnp.where(at_oxidizer, oxidizer_state, new_populations)

    lattice, lweights, lreverse = species_tables()
    count = species.shape[1]
    labels = jnp.arange(count, dtype=jnp.int32)[None]
    first_hot = (reactions[:, 0:1] == labels).astype(jnp.float32)
    second_hot = (reactions[:, 1:2] == labels).astype(jnp.float32)
    product_hot = (reactions[:, 2:3] == labels).astype(jnp.float32)
    stoich = (product_hot - first_hot - second_hot).T
    along = (column(component(lattice, 0), 4) * flow_x[None, None] + column(component(lattice, 1), 4) * flow_y[None, None]
             + column(component(lattice, 2), 4) * flow_z[None, None])
    lattice_weights = column(lweights, 4)
    relax = species_rate.reshape(1, -1, 1, 1, 1)
    fuel_species = lattice_weights * inlet_mix[0].reshape(1, -1, 1, 1, 1) * (1.0 + 4.0 * inlet_speed * column(component(lattice, 1), 4))
    oxidizer_species = lattice_weights * inlet_mix[1].reshape(1, -1, 1, 1, 1) * (1.0 - 4.0 * inlet_speed * column(component(lattice, 1), 4))
    expanded = [entry for entry in lattice for copy_index in range(count)]
    reverse_index = jnp.asarray(lreverse, jnp.int32)
    for substep in range(SUBSTEPS):
        conc = jnp.sum(species, 0)
        flat = conc.reshape(count, -1)
        first_conc = jnp.dot(first_hot, flat, precision=high)
        second_conc = jnp.dot(second_hot, flat, precision=high)
        rates = rate_const[:, None] * first_conc * second_conc
        source = jnp.dot(stoich, rates, precision=high).reshape(conc.shape)
        balance = lattice_weights * conc[None] * (1.0 + 4.0 * along)
        gpost = species + relax * (balance - species) + lattice_weights * source[None]
        shape = gpost.shape
        moved_species = stream(gpost.reshape((shape[0] * shape[1],) + shape[2:]), expanded).reshape(shape)
        species = jnp.where(is_wall[None], moved_species[reverse_index], moved_species)
        species = jnp.where(at_fuel[None], fuel_species, species)
        species = jnp.where(at_oxidizer[None], oxidizer_species, species)
    return new_populations, species
```

```python
import functools

import jax
import jax.numpy as jnp
from jax import lax
from jax.experimental import pallas as pl
from jax.experimental.pallas import tpu as pltpu
from jax.sharding import PartitionSpec as P

SUBSTEPS = 3
OMEGA = 1.6
SPEED = 0.05
F32 = jnp.float32
BF16 = jnp.bfloat16
VEL = [(a, b, c) for a in (-1, 0, 1) for b in (-1, 0, 1) for c in (-1, 0, 1)]
WT = [(8.0 / 27, 2.0 / 27, 1.0 / 54, 1.0 / 216)[abs(a) + abs(b) + abs(c)] for a, b, c in VEL]
UPX = [q for q in range(27) if VEL[q][0] > 0]
DNX = [q for q in range(27) if VEL[q][0] < 0]
UPY = [q for q in range(27) if VEL[q][1] > 0]
DNY = [q for q in range(27) if VEL[q][1] < 0]
MIB = 1 << 20
VMEM = pltpu.VMEM
VM = pl.BlockSpec(memory_space=pltpu.VMEM)
SM = pl.BlockSpec(memory_space=pltpu.SMEM)
ANY = pl.BlockSpec(memory_space=pl.ANY)


def inv(x):
    return pltpu.with_memory_space_constraint(x, pltpu.VMEM)


def ring(size, step):
    return [(i, (i + step) % size) for i in range(size)]


def call(body, name, ins, specs, outs, out_specs, scratch=(), alias=None, mib=12, cost=2_000_000):
    return pl.pallas_call(
        body,
        name=name,
        out_shape=outs,
        in_specs=specs,
        out_specs=out_specs,
        scratch_shapes=list(scratch),
        input_output_aliases=alias or {},
        compiler_params=pltpu.CompilerParams(vmem_limit_bytes=mib * MIB),
        cost_estimate=pl.CostEstimate(flops=cost, bytes_accessed=cost, transcendentals=0),
    )(*ins)


def react(rx, kc, c_ref, s_ref, w_ref, rt_ref):
    species, rows, lanes = c_ref.shape
    tiles = rows // 8
    half = rt_ref.shape[0] // 2

    def pair(i, carry):
        rates = []
        for n in range(2):
            j = 2 * i + n
            rates.append(c_ref[rx[3 * j]] * c_ref[rx[3 * j + 1]] * kc[j])
        for t in range(tiles):
            both = jnp.concatenate([r[8 * t : 8 * t + 8] for r in rates], axis=0)
            high = both.astype(BF16)
            low = (both - high.astype(F32)).astype(BF16)
            rt_ref[pl.ds(pl.multiple_of(16 * i, 16), 16), lanes * t : lanes * (t + 1)] = high
            rt_ref[pl.ds(pl.multiple_of(half + 16 * i, 16), 16), lanes * t : lanes * (t + 1)] = low
        return carry

    lax.fori_loop(0, half // 16, pair, 0, unroll=3)
    total = jnp.dot(w_ref[...], rt_ref[...], preferred_element_type=F32)
    for t in range(tiles):
        s_ref[:, 8 * t : 8 * t + 8, :] = total[:, lanes * t : lanes * (t + 1)].reshape(
            species, 8, lanes
        )


def moments(f):
    rho = f[0]
    for q in range(1, 27):
        rho = rho + f[q]
    parts = []
    for axis in range(3):
        plus = None
        for q in range(27):
            if VEL[q][axis] > 0:
                diff = f[q] - f[26 - q]
                plus = diff if plus is None else plus + diff
        parts.append(plus)
    scale = 1.0 / rho
    return rho, [p * scale for p in parts]


def cross(g, rk, c, s, ux, sign):
    a = rk * c
    return (1.0 - rk) * g + (0.125 * (a + s) + (0.5 * sign) * (a * ux))


def first_body(pop, spec, rx, kc, rk, w, pv, sv, mu, md, c03, s03, rt, psem, ssem):
    planes, rows = pop.shape[1], pop.shape[2]
    species = spec.shape[1]
    order = [0, planes - 1] + list(range(1, planes - 1))
    copies = {}
    for x in order[:2]:
        copies["s", x] = pltpu.make_async_copy(spec.at[:, :, x], sv.at[:, :, x], ssem.at[x])
        copies["p", x] = pltpu.make_async_copy(pop.at[:, x], pv.at[:, x], psem.at[x])
    for x in order[2:]:
        copies["p", x] = pltpu.make_async_copy(pop.at[:, x], pv.at[:, x], psem.at[x])
        copies["s", x] = pltpu.make_async_copy(spec.at[:, :, x], sv.at[:, :, x], ssem.at[x])
    for copy in copies.values():
        copy.start()
    for n, x in enumerate(order[:2]):
        copies["s", x].wait()

        def conc(k, carry, n=n, x=x):
            total = sv[0, k, x]
            for i in range(1, 7):
                total = total + sv[i, k, x]
            c03[k, n * rows : (n + 1) * rows, :] = total
            return carry

        lax.fori_loop(0, species, conc, 0, unroll=5)
    react(rx, kc, c03, s03, w, rt)
    for n, x in enumerate(order[:2]):
        copies["p", x].wait()
        _, (ux, _, _) = moments([pv[q, x] for q in range(27)])
        out, i, sign = ((md, 2, -1.0), (mu, 1, 1.0))[n]

        def send(k, carry, n=n, x=x, out=out, i=i, sign=sign, ux=ux):
            half = slice(n * rows, (n + 1) * rows)
            out[k] = cross(sv[i, k, x], rk[k], c03[k, half, :], s03[k, half, :], ux, sign)
            return carry

        lax.fori_loop(0, species, send, 0, unroll=5)
    for x in order[2:]:
        copies["p", x].wait()
        copies["s", x].wait()


def flow_body(pv, u, post, fu, fd):
    planes = pv.shape[1]
    for x in range(planes):
        f = [pv[q, x] for q in range(27)]
        rho, v = moments(f)
        for axis in range(3):
            u[axis, x] = v[axis]
        still = 1.0 - 1.5 * (v[0] * v[0] + v[1] * v[1] + v[2] * v[2])
        scaled = OMEGA * rho
        post[13, x] = (1.0 - OMEGA) * f[13] + WT[13] * scaled * still
        for q in range(14, 27):
            along = None
            for axis in range(3):
                if VEL[q][axis]:
                    term = v[axis] if VEL[q][axis] > 0 else -v[axis]
                    along = term if along is None else along + term
            even = still + 4.5 * along * along
            odd = 3.0 * along
            ws = WT[q] * scaled
            for p, value in ((q, even + odd), (26 - q, even - odd)):
                out = (1.0 - OMEGA) * f[p] + ws * value
                post[p, x] = out
                if x == planes - 1 and p in UPX:
                    fu[UPX.index(p)] = out
                if x == 0 and p in DNX:
                    fd[DNX.index(p)] = out


def row_index(rows, lanes):
    return lax.broadcasted_iota(jnp.int32, (rows, lanes), 0)


def gather(k, x, g, hxu, hxd, hyu, hyd, pairs):
    planes, rows, lanes = g.shape[2:]
    out = {}
    if 0 in pairs:
        out[0] = g[0, k, x]
    if 1 in pairs:
        out[1] = g[1, k, x - 1] if x > 0 else hxu[k]
        out[2] = g[2, k, x + 1] if x < planes - 1 else hxd[k]
    if 3 in pairs:
        at = row_index(rows, lanes)
        spot = pl.ds(k * planes + x, 1)
        out[3] = jnp.where(at == 0, hyu[spot, :], pltpu.roll(g[3, k, x], 1, 0))
        out[4] = jnp.where(at == rows - 1, hyd[spot, :], pltpu.roll(g[4, k, x], rows - 1, 0))
    if 5 in pairs:
        out[5] = pltpu.roll(g[5, k, x], 1, 1)
        out[6] = pltpu.roll(g[6, k, x], lanes - 1, 1)
    return out


def bounded(moved, nt, mix, k, species):
    wall = nt == 1
    inlet = nt >= 2
    fuel = nt == 2
    value = jnp.where(fuel, mix[k], mix[species + k])
    out = {}
    for i, m in moved.items():
        r = (0, 2, 1, 4, 3, 6, 5)[i]
        other = m if i == 0 else jnp.where(wall, moved[r], m)
        if i == 0:
            fixed = 0.25 * value
        elif i in (3, 4):
            tilt = 4.0 * SPEED * (1.0 if i == 3 else -1.0)
            fixed = jnp.where(fuel, 0.125 * (1.0 + tilt), 0.125 * (1.0 - tilt)) * value
        else:
            fixed = 0.125 * value
        out[i] = jnp.where(inlet, fixed, other)
    return out


def edge_body(g, hxu, hxd, hyu, hyd, nt, u, rx, kc, rk, mix, w, new, mu, md, c03, s03, rt):
    planes, rows = g.shape[2], g.shape[3]
    species = g.shape[1]
    ends = (0, planes - 1)
    for n, x in enumerate(ends):
        kind = nt[x]

        def step(k, carry, n=n, x=x, kind=kind):
            values = bounded(
                gather(k, x, g, hxu, hxd, hyu, hyd, (0, 1, 3, 5)), kind, mix, k, species
            )
            total = None
            for i in range(7):
                new[i, k, x] = values[i]
                total = values[i] if total is None else total + values[i]
            c03[k, n * rows : (n + 1) * rows, :] = total
            return carry

        lax.fori_loop(0, species, step, 0, unroll=4)
    react(rx, kc, c03, s03, w, rt)
    for n, x in enumerate(ends):
        ux = u[0, x]
        out, i, sign = ((md, 2, -1.0), (mu, 1, 1.0))[n]

        def send(k, carry, n=n, x=x, out=out, i=i, sign=sign, ux=ux):
            half = slice(n * rows, (n + 1) * rows)
            out[k] = cross(new[i, k, x], rk[k], c03[k, half, :], s03[k, half, :], ux, sign)
            return carry

        lax.fori_loop(0, species, send, 0, unroll=5)


def rest_body(moving, flow, *refs):
    refs = list(refs)
    g = refs.pop(0) if moving else None
    start, c03, s03, u, rx, kc, rk, w = [refs.pop(0) for _ in range(8)]
    if moving:
        hyu, hyd, nt, mix = [refs.pop(0) for _ in range(4)]
    if flow:
        post, fhu, fhd = [refs.pop(0) for _ in range(3)]
    new, yu, yd, c12, s12, rt = refs
    species, planes, rows, lanes = new.shape[1:]
    for x in range(1, planes - 1):
        kind = nt[x] if moving else None

        def step(k, carry, x=x, kind=kind):
            if moving:
                values = bounded(
                    gather(k, x, g, None, None, hyu, hyd, (0, 1, 3, 5)), kind, mix, k, species
                )
            else:
                values = {i: start[i, k, x] for i in range(7)}
            total = None
            for i in range(7):
                if moving:
                    new[i, k, x] = values[i]
                total = values[i] if total is None else total + values[i]
            c12[k, (x - 1) * rows : x * rows, :] = total
            return carry

        lax.fori_loop(0, species, step, 0, unroll=4)
    react(rx, kc, c12, s12, w, rt)
    first = lax.axis_index("gy") == 0
    last = lax.axis_index("gy") == lax.axis_size("gy") - 1
    for x in range(planes):
        ux, uy, uz = u[0, x], u[1, x], u[2, x]
        if x in (0, planes - 1):
            cr, sr, half = c03, s03, slice((x > 0) * rows, (x > 0) * rows + rows)
        else:
            cr, sr, half = c12, s12, slice((x - 1) * rows, x * rows)

        def collide(k, carry, x=x, cr=cr, sr=sr, half=half, ux=ux, uy=uy, uz=uz):
            r = rk[k]
            keep = 1.0 - r
            a = r * cr[k, half, :]
            base = a + sr[k, half, :]
            base1 = 0.125 * base
            lean = 0.5 * a
            new[0, k, x] = keep * new[0, k, x] + 0.25 * base
            for i, v in ((1, ux), (3, uy), (5, uz)):
                d = lean * v
                up = keep * new[i, k, x] + (base1 + d)
                down = keep * new[i + 1, k, x] + (base1 - d)
                new[i, k, x] = up
                new[i + 1, k, x] = down
                if i == 3:
                    spot = pl.ds(k * planes + x, 1)
                    yu[spot, :] = jnp.where(last, 0.0, up[rows - 1 : rows])
                    yd[spot, :] = jnp.where(first, 0.0, down[0:1])
            return carry

        lax.fori_loop(0, species, collide, 0, unroll=4)
    if flow:
        for n, q in enumerate(UPY):
            for x in range(planes):
                at = species * planes + n * planes + x
                row = flow_rows(q, x, post, fhu, fhd)[rows - 1 : rows]
                yu[at : at + 1, :] = jnp.where(last, 0.0, row)
        for n, q in enumerate(DNY):
            for x in range(planes):
                at = species * planes + n * planes + x
                row = flow_rows(q, x, post, fhu, fhd)[0:1]
                yd[at : at + 1, :] = jnp.where(first, 0.0, row)


def flow_rows(q, x, post, fhu, fhd):
    planes = post.shape[1]
    src = x - VEL[q][0]
    if src < 0:
        return fhu[UPX.index(q)]
    if src >= planes:
        return fhd[DNX.index(q)]
    return post[q, src]


def flow_end_body(base, post, fhu, fhd, hyu, hyd, nt, out):
    planes, rows, lanes = post.shape[1:]
    at = row_index(rows, lanes)
    for x in range(planes):
        kind = nt[x]
        wall = kind == 1
        inlet = kind >= 2
        fuel = kind == 2
        for q in range(13, 27):
            moved = {}
            for p in {q, 26 - q}:
                a, b, c = VEL[p]
                value = flow_rows(p, x, post, fhu, fhd)
                if b > 0:
                    spot = base + UPY.index(p) * planes + x
                    value = jnp.where(at == 0, hyu[spot : spot + 1, :], pltpu.roll(value, 1, 0))
                elif b < 0:
                    spot = base + DNY.index(p) * planes + x
                    value = jnp.where(
                        at == rows - 1, hyd[spot : spot + 1, :], pltpu.roll(value, rows - 1, 0)
                    )
                if c:
                    value = pltpu.roll(value, 1 if c > 0 else lanes - 1, 1)
                moved[p] = value
            for p in moved:
                cu = VEL[p][1] * SPEED
                fixed = [
                    WT[p] * (1.0 + 3.0 * s * cu + 4.5 * cu * cu - 1.5 * SPEED * SPEED)
                    for s in (1.0, -1.0)
                ]
                value = moved[p] if p == 13 else jnp.where(wall, moved[26 - p], moved[p])
                out[p, x] = jnp.where(inlet, jnp.where(fuel, fixed[0], fixed[1]), value)


def end_body(g, hyu, hyd, nt, mix, out):
    step = pl.program_id(0)
    planes = g.shape[2]
    species = g.shape[1]
    chunk = out.shape[1]
    for n in range(chunk):
        k = step * chunk + n
        for x in range(planes):
            pairs = (0, 1, 3, 5) if 0 < x < planes - 1 else (0, 3, 5)
            values = bounded(gather(k, x, g, None, None, hyu, hyd, pairs), nt[x], mix, k, species)
            for i, value in values.items():
                out[i, n, x] = value


def final_body(g, hxu, hxd, nt, mix, before, out, buf, sem):
    del before
    planes = g.shape[2]
    species = g.shape[1]
    copies = []
    for n, x in enumerate((0, planes - 1)):
        kind = nt[x]

        def step(k, carry, n=n, x=x, kind=kind):
            values = bounded(gather(k, x, g, hxu, hxd, None, None, (1,)), kind, mix, k, species)
            for i in (1, 2):
                buf[2 * n + i - 1, k] = values[i]
            return carry

        lax.fori_loop(0, species, step, 0, unroll=5)
        for i in (1, 2):
            copy = pltpu.make_async_copy(
                buf.at[2 * n + i - 1], out.at[i, :, x], sem.at[2 * n + i - 1]
            )
            copy.start()
            copies.append(copy)
    for copy in copies:
        copy.wait()


def per_device(populations, species, node_type, reactions, rate_const, species_rate, inlet_mix):
    planes, rows, lanes = node_type.shape
    count = species.shape[1]
    total = reactions.shape[0]
    pad = total % 2
    if pad:
        reactions = jnp.pad(reactions, ((0, pad), (0, 0)))
        rate_const = jnp.pad(rate_const, (0, pad))
        total += pad
    labels = jnp.arange(count, dtype=jnp.int32)[:, None]
    hot = [(reactions[:, n][None] == labels).astype(F32) for n in range(3)]
    stoich = hot[2] - hot[0] - hot[1]
    w = jnp.kron(stoich, jnp.eye(8, dtype=F32)).astype(BF16)
    w = inv(jnp.concatenate([w, w], axis=1))
    rx = reactions.reshape(-1)
    mix = inlet_mix.reshape(-1)
    nt = inv(node_type)

    def arr(*shape):
        return VMEM(shape, F32)

    state = arr(7, count, planes, rows, lanes)
    xmsg = arr(count, rows, lanes)
    react_out = arr(count, 2 * rows, lanes)
    inner = planes - 2
    tiles = rows // 8
    rates = VMEM((2 * total * 8, 2 * tiles * lanes), BF16)
    rates_in = VMEM((2 * total * 8, inner * tiles * lanes), BF16)
    inside = VMEM((count, inner * rows, lanes), F32)

    pv, sv, mu, md, c03, s03 = call(
        first_body,
        "first",
        (populations, species, rx, rate_const, species_rate, w),
        [ANY, ANY, SM, SM, SM, VM],
        (arr(27, planes, rows, lanes), state, xmsg, xmsg, react_out, react_out),
        [VM] * 6,
        [rates, pltpu.SemaphoreType.DMA((planes,)), pltpu.SemaphoreType.DMA((planes,))],
    )

    def swap_x(up, down):
        size = lax.axis_size("gx")
        return lax.ppermute(up, "gx", ring(size, 1)), lax.ppermute(down, "gx", ring(size, -1))

    def swap_y(up, down):
        size = lax.axis_size("gy")
        return lax.ppermute(up, "gy", ring(size, 1)), lax.ppermute(down, "gy", ring(size, -1))

    hxu, hxd = swap_x(mu, md)
    fmsg = arr(9, rows, lanes)
    u, post, fu, fd = call(
        flow_body,
        "flow",
        (inv(pv),),
        [VM],
        (arr(3, planes, rows, lanes), arr(27, planes, rows, lanes), fmsg, fmsg),
        [VM] * 4,
    )
    fhu, fhd = swap_x(fu, fd)

    g = None
    new = sv
    for s in range(SUBSTEPS):
        moving, flow = s > 0, s == 1
        if moving:
            new, mu, md, c03, s03 = call(
                edge_body,
                f"edge{s}",
                (inv(g), inv(hxu), inv(hxd), inv(hyu), inv(hyd), nt, inv(u), rx, rate_const,
                 species_rate, mix, w),
                [VM] * 7 + [SM] * 4 + [VM],
                (state, xmsg, xmsg, react_out, react_out),
                [VM] * 5,
                [rates],
            )
            hxu, hxd = swap_x(mu, md)
        height = count * planes + (9 * planes if flow else 0)
        ymsg = arr(height, lanes)
        ins = ([inv(g)] if moving else []) + [
            inv(new), inv(c03), inv(s03), inv(u), rx, rate_const, species_rate, w
        ]
        specs = ([VM] if moving else []) + [VM] * 4 + [SM] * 3 + [VM]
        if moving:
            ins += [inv(hyu), inv(hyd), nt, mix]
            specs += [VM, VM, VM, SM]
        if flow:
            ins += [inv(post), inv(fhu), inv(fhd)]
            specs += [VM] * 3
        g, yu, yd = call(
            functools.partial(rest_body, moving, flow),
            f"rest{s}",
            ins,
            specs,
            (state, ymsg, ymsg),
            [VM] * 3,
            [inside, inside, rates_in],
            alias={1 if moving else 0: 0},
        )
        hyu, hyd = swap_y(yu, yd)
        if flow:
            new_populations = call(
                functools.partial(flow_end_body, count * planes),
                "flow_end",
                (inv(post), inv(fhu), inv(fhd), inv(hyu), inv(hyd), nt),
                [VM] * 6,
                jax.ShapeDtypeStruct((27, planes, rows, lanes), F32),
                VM,
            )
    chunk = 2 if count % 2 == 0 else 1
    shape = jax.ShapeDtypeStruct((7, count, planes, rows, lanes), F32)
    new_species = pl.pallas_call(
        end_body,
        name="end",
        grid=(count // chunk,),
        out_shape=shape,
        in_specs=[VM] * 4 + [SM],
        out_specs=pl.BlockSpec((7, chunk, planes, rows, lanes), lambda i: (0, i, 0, 0, 0)),
        compiler_params=pltpu.CompilerParams(vmem_limit_bytes=12 * MIB),
        cost_estimate=pl.CostEstimate(flops=2_000_000, bytes_accessed=9_000_000, transcendentals=0),
    )(inv(g), inv(hyu), inv(hyd), nt, mix)
    new_species = call(
        final_body,
        "final",
        (inv(g), inv(hxu), inv(hxd), nt, mix, new_species),
        [VM] * 4 + [SM, ANY],
        shape,
        ANY,
        [VMEM((4, count, rows, lanes), F32), pltpu.SemaphoreType.DMA((4,))],
        alias={5: 0},
    )
    return new_populations, new_species


def solution(mesh):
    flow = P(None, "gx", "gy", None)
    kinds = P(None, None, "gx", "gy", None)
    return jax.shard_map(
        per_device,
        mesh=mesh,
        in_specs=(flow, kinds, P("gx", "gy", None), P(), P(), P(), P()),
        out_specs=(flow, kinds),
        check_vma=False,
    )
```

```python
import functools

import jax
import jax.numpy as jnp
from jax import lax
from jax.experimental import pallas as pl
from jax.experimental.pallas import tpu as pltpu
from jax.sharding import PartitionSpec as P

SUBSTEPS = 3
OMEGA = 1.6
SPEED = 0.05
F32 = jnp.float32
BF16 = jnp.bfloat16
VEL = [(a, b, c) for a in (-1, 0, 1) for b in (-1, 0, 1) for c in (-1, 0, 1)]
WT = [(8.0 / 27, 2.0 / 27, 1.0 / 54, 1.0 / 216)[abs(a) + abs(b) + abs(c)] for a, b, c in VEL]
UPX = [q for q in range(27) if VEL[q][0] > 0]
DNX = [q for q in range(27) if VEL[q][0] < 0]
UPY = [q for q in range(27) if VEL[q][1] > 0]
DNY = [q for q in range(27) if VEL[q][1] < 0]
MIB = 1 << 20
VMEM = pltpu.VMEM
VM = pl.BlockSpec(memory_space=pltpu.VMEM)
SM = pl.BlockSpec(memory_space=pltpu.SMEM)
ANY = pl.BlockSpec(memory_space=pl.ANY)


def inv(x):
    return pltpu.with_memory_space_constraint(x, pltpu.VMEM)


def hbm(x):
    return pltpu.with_memory_space_constraint(x, pltpu.HBM)


def ring(size, step):
    return [(i, (i + step) % size) for i in range(size)]


def call(body, name, ins, specs, outs, out_specs, scratch=(), alias=None, mib=12, cost=2_000_000):
    return pl.pallas_call(
        body,
        name=name,
        out_shape=outs,
        in_specs=specs,
        out_specs=out_specs,
        scratch_shapes=list(scratch),
        input_output_aliases=alias or {},
        compiler_params=pltpu.CompilerParams(vmem_limit_bytes=mib * MIB),
        cost_estimate=pl.CostEstimate(flops=cost, bytes_accessed=cost, transcendentals=0),
    )(*ins)


def react(rx, kc, c_ref, s_ref, w_ref, rt_ref):
    species, rows, lanes = c_ref.shape
    tiles = rows // 8
    half = rt_ref.shape[0] // 2

    def pair(i, carry):
        rates = []
        for n in range(2):
            j = 2 * i + n
            rates.append(c_ref[rx[0, j]] * c_ref[rx[1, j]] * kc[j])
        for t in range(tiles):
            both = jnp.concatenate([r[8 * t : 8 * t + 8] for r in rates], axis=0)
            high = both.astype(BF16)
            low = (both - high.astype(F32)).astype(BF16)
            rt_ref[pl.ds(pl.multiple_of(16 * i, 16), 16), lanes * t : lanes * (t + 1)] = high
            rt_ref[pl.ds(pl.multiple_of(half + 16 * i, 16), 16), lanes * t : lanes * (t + 1)] = low
        return carry

    lax.fori_loop(0, half // 16, pair, 0, unroll=3)
    total = jnp.dot(w_ref[...], rt_ref[...], preferred_element_type=F32)
    for t in range(tiles):
        s_ref[:, 8 * t : 8 * t + 8, :] = total[:, lanes * t : lanes * (t + 1)].reshape(
            species, 8, lanes
        )


def moments(f):
    rho = f[0]
    for q in range(1, 27):
        rho = rho + f[q]
    parts = []
    for axis in range(3):
        plus = None
        for q in range(27):
            if VEL[q][axis] > 0:
                diff = f[q] - f[26 - q]
                plus = diff if plus is None else plus + diff
        parts.append(plus)
    scale = 1.0 / rho
    return rho, [p * scale for p in parts]


def cross(g, rk, c, s, ux, sign):
    a = rk * c
    return (1.0 - rk) * g + (0.125 * (a + s) + (0.5 * sign) * (a * ux))


def bands(species):
    return [(k, min(8, species - k)) for k in range(0, species, 8)]


def stoichiometry(rv, w):
    rows, width = w.shape
    half = width // 2
    species, total = rows // 8, half // 8

    def iota(shape, axis):
        return lax.broadcasted_iota(jnp.int32, shape, axis)

    def hot(test):
        return jnp.where(test, 1.0, 0.0)

    label = iota((species, total), 0)
    net = hot(rv[2:3, :] == label) - hot(rv[0:1, :] == label) - hot(rv[1:2, :] == label)
    tall = hot((iota((rows, species), 0) >> 3) == iota((rows, species), 1)).astype(BF16)
    wide = hot((iota((total, half), 1) >> 3) == iota((total, half), 0)).astype(BF16)
    part = jnp.dot(tall, net.astype(BF16), preferred_element_type=F32)
    full = jnp.dot(part.astype(BF16), wide, preferred_element_type=F32)
    same = (iota((rows, half), 0) & 7) == (iota((rows, half), 1) & 7)
    full = jnp.where(same, full, 0.0).astype(BF16)
    w[:, :half] = full
    w[:, half:] = full


def first_body(pop, spec, rv, rx, kc, rk, mix, pv, sv, w, mu, md, c03, s03, fixed, rt, psem, ssem):
    planes, rows, lanes = pop.shape[1:]
    species = spec.shape[1]
    order = [0, planes - 1] + list(range(1, planes - 1))
    copies = {}
    for x in order[:2]:
        copies["s", x] = pltpu.make_async_copy(spec.at[:, :, x], sv.at[:, :, x], ssem.at[x])
    for x in order:
        copies["p", x] = pltpu.make_async_copy(pop.at[:, x], pv.at[:, x], psem.at[x])
    for x in order[2:]:
        copies["s", x] = pltpu.make_async_copy(spec.at[:, :, x], sv.at[:, :, x], ssem.at[x])
    for copy in copies.values():
        copy.start()
    stoichiometry(rv, w)
    for k in range(species):
        for n, value in enumerate((rk[k], mix[0, k], mix[1, k])):
            fixed[n, k : k + 1, :] = jnp.full((1, lanes), value, F32)
    for n, x in enumerate(order[:2]):
        copies["s", x].wait()

        def conc(k, carry, n=n, x=x):
            total = sv[0, k, x]
            for i in range(1, 7):
                total = total + sv[i, k, x]
            c03[k, n * rows : (n + 1) * rows, :] = total
            return carry

        lax.fori_loop(0, species, conc, 0, unroll=5)
    if c03.shape[1] > 2 * rows:
        rest = c03.shape[1] - 2 * rows
        for k in range(species):
            c03[k, 2 * rows :, :] = jnp.zeros((rest, lanes), F32)
    react(rx, kc, c03, s03, w, rt)
    for n, x in enumerate(order[:2]):
        copies["p", x].wait()
        f = [pv[q, x] for q in range(27)]
        rho, v = moments(f)
        ux = v[0]
        out, i, sign = ((md, 2, -1.0), (mu, 1, 1.0))[n]

        def send(k, carry, n=n, x=x, out=out, i=i, sign=sign, ux=ux):
            half = slice(n * rows, (n + 1) * rows)
            out[k] = cross(sv[i, k, x], rk[k], c03[k, half, :], s03[k, half, :], ux, sign)
            return carry

        lax.fori_loop(0, species, send, 0, unroll=5)
        for m, q in enumerate((DNX, UPX)[n]):
            still, scaled, (even, odd) = relaxed(rho, v, q)
            out[species + m] = (1.0 - OMEGA) * f[q] + WT[q] * scaled * (even + odd)
    for x in order[2:]:
        copies["p", x].wait()
        copies["s", x].wait()


def relaxed(rho, v, q):
    still = 1.0 - 1.5 * (v[0] * v[0] + v[1] * v[1] + v[2] * v[2])
    along = None
    for axis in range(3):
        if VEL[q][axis]:
            term = v[axis] if VEL[q][axis] > 0 else -v[axis]
            along = term if along is None else along + term
    return still, OMEGA * rho, (still + 4.5 * along * along, 3.0 * along)


def flow_body(pv, u, post):
    planes = pv.shape[1]
    for x in range(planes):
        f = [pv[q, x] for q in range(27)]
        rho, v = moments(f)
        for axis in range(3):
            u[axis, x] = v[axis]
        for q in range(14, 27):
            still, scaled, (even, odd) = relaxed(rho, v, q)
            ws = WT[q] * scaled
            for p, value in ((q, even + odd), (26 - q, even - odd)):
                post[p, x] = (1.0 - OMEGA) * f[p] + ws * value
        post[13, x] = (1.0 - OMEGA) * f[13] + WT[13] * scaled * still


def row_index(rows, lanes):
    return lax.broadcasted_iota(jnp.int32, (rows, lanes), 0)


def gather(k, x, g, hxu, hxd, hyu, hyd, pairs):
    planes, rows, lanes = g.shape[2:]
    out = {}
    if 0 in pairs:
        out[0] = g[0, k, x]
    if 1 in pairs:
        out[1] = g[1, k, x - 1] if x > 0 else hxu[k]
        out[2] = g[2, k, x + 1] if x < planes - 1 else hxd[k]
    if 3 in pairs:
        at = row_index(rows, lanes)
        spot = pl.ds(x * g.shape[1] + k, 1)
        out[3] = jnp.where(at == 0, hyu[spot, :], pltpu.roll(g[3, k, x], 1, 0))
        out[4] = jnp.where(at == rows - 1, hyd[spot, :], pltpu.roll(g[4, k, x], rows - 1, 0))
    if 5 in pairs:
        out[5] = pltpu.roll(g[5, k, x], 1, 1)
        out[6] = pltpu.roll(g[6, k, x], lanes - 1, 1)
    return out


def bounded(moved, nt, mix, k, species):
    wall = nt == 1
    inlet = nt >= 2
    fuel = nt == 2
    return bounce(moved, wall, inlet, fuel, jnp.where(fuel, mix[0, k], mix[1, k]))


def bounce(moved, wall, inlet, fuel, value):
    out = {}
    for i, m in moved.items():
        r = (0, 2, 1, 4, 3, 6, 5)[i]
        other = m if i == 0 else jnp.where(wall, moved[r], m)
        if i == 0:
            fixed = 0.25 * value
        elif i in (3, 4):
            tilt = 4.0 * SPEED * (1.0 if i == 3 else -1.0)
            fixed = jnp.where(fuel, 0.125 * (1.0 + tilt), 0.125 * (1.0 - tilt)) * value
        else:
            fixed = 0.125 * value
        out[i] = jnp.where(inlet, fixed, other)
    return out


def edge_body(flow, *refs):
    refs = list(refs)
    g, hxu, hxd, hyu, hyd, nt, u, rx, kc, rk, mix, w, fixed = [refs.pop(0) for _ in range(13)]
    post = refs.pop(0) if flow else None
    new, mu, md, yu, yd, c03, s03, rt = refs
    species, planes, rows, lanes = g.shape[1:]
    height = c03.shape[1]
    ends = (0, planes - 1)
    flat = g.reshape(7 * species * planes * rows, lanes)
    fresh = new.reshape(7 * species * planes * rows, lanes)
    cflat = c03.reshape(species * height, lanes)
    sflat = s03.reshape(species * height, lanes)
    jump = planes * rows
    zeros = height - 2 * rows
    for k in range(species):
        c03[k, 2 * rows :, :] = jnp.zeros((zeros, lanes), F32)
    for x in range(1, planes - 1):
        for side, row in ((0, 0), (1, rows - 1)):
            kind = nt[x, row : row + 1, :]
            wall, inlet, fuel = kind == 1, kind >= 2, kind == 2
            for k, size in bands(species):

                def load(i, plane, r, k=k, size=size):
                    return flat[pl.ds(((i * species + k) * planes + plane) * rows + r, size, jump), :]

                halo = slice(x * species + k, x * species + k + size)
                moved = {
                    0: load(0, x, row),
                    1: load(1, x - 1, row),
                    2: load(2, x + 1, row),
                    3: hyu[halo, :] if side == 0 else load(3, x, row - 1),
                    4: hyd[halo, :] if side == 1 else load(4, x, row + 1),
                    5: pltpu.roll(load(5, x, row), 1, 1),
                    6: pltpu.roll(load(6, x, row), lanes - 1, 1),
                }
                wide = [jnp.broadcast_to(m, (size, lanes)) for m in (wall, inlet, fuel)]
                value = jnp.where(wide[2], fixed[1, k : k + size, :], fixed[2, k : k + size, :])
                values = bounce(moved, *wide, value)
                total = None
                for i in range(7):
                    total = values[i] if total is None else total + values[i]
                spot = 2 * rows + 2 * (x - 1) + side
                cflat[pl.ds(k * height + spot, size, height), :] = total
                if side:
                    yu[halo, :] = values[3]
                else:
                    yd[halo, :] = values[4]
    for n, x in enumerate(ends):
        kind = nt[x]

        def step(k, carry, n=n, x=x, kind=kind):
            values = bounded(
                gather(k, x, g, hxu, hxd, hyu, hyd, (0, 1, 3, 5)), kind, mix, k, species
            )
            total = None
            for i in range(7):
                new[i, k, x] = values[i]
                total = values[i] if total is None else total + values[i]
            c03[k, n * rows : (n + 1) * rows, :] = total
            return carry

        lax.fori_loop(0, species, step, 0, unroll=4)
    react(rx, kc, c03, s03, w, rt)
    for n, x in enumerate(ends):
        ux = u[0, x]
        out, i, sign = ((md, 2, -1.0), (mu, 1, 1.0))[n]

        def send(k, carry, n=n, x=x, out=out, i=i, sign=sign, ux=ux):
            half = slice(n * rows, (n + 1) * rows)
            out[k] = cross(new[i, k, x], rk[k], c03[k, half, :], s03[k, half, :], ux, sign)
            return carry

        lax.fori_loop(0, species, send, 0, unroll=5)
    first = lax.axis_index("gy") == 0
    last = lax.axis_index("gy") == lax.axis_size("gy") - 1
    for x in range(planes):
        for side, row in ((0, 0), (1, rows - 1)):
            uy = u[1, x, row : row + 1, :]
            out, i, sign, off = ((yd, 4, -1.0, first), (yu, 3, 1.0, last))[side]
            if x in ends:
                spot = (x > 0) * rows + row
            else:
                spot = 2 * rows + 2 * (x - 1) + side
            for k, size in bands(species):
                halo = slice(x * species + k, x * species + k + size)
                if x in ends:
                    at = ((i * species + k) * planes + x) * rows + row
                    value = fresh[pl.ds(at, size, jump), :]
                else:
                    value = out[halo, :]
                c = cflat[pl.ds(k * height + spot, size, height), :]
                s = sflat[pl.ds(k * height + spot, size, height), :]
                value = cross(value, fixed[0, k : k + size, :], c, s, uy, sign)
                out[halo, :] = jnp.where(off, 0.0, value)
    if flow:
        base = species * planes
        for out, queue, row, off in ((yu, UPY, rows - 1, last), (yd, DNY, 0, first)):
            for n, q in enumerate(queue):
                for x in range(planes):
                    at = base + n * planes + x
                    value = flow_rows(q, x, post, hxu, hxd, species, slice(row, row + 1))
                    out[at : at + 1, :] = jnp.where(off, 0.0, value)


def rest_body(moving, *refs):
    refs = list(refs)
    g = refs.pop(0) if moving else None
    start, c03, s03, u, rx, kc, rk, w = [refs.pop(0) for _ in range(8)]
    if moving:
        hyu, hyd, nt, mix = [refs.pop(0) for _ in range(4)]
    new = refs.pop(0)
    if not moving:
        yu, yd = [refs.pop(0) for _ in range(2)]
    c12, s12, rt = refs
    species, planes, rows, lanes = new.shape[1:]
    for x in range(1, planes - 1):
        kind = nt[x] if moving else None

        def step(k, carry, x=x, kind=kind):
            if moving:
                values = bounded(
                    gather(k, x, g, None, None, hyu, hyd, (0, 1, 3, 5)), kind, mix, k, species
                )
            else:
                values = {i: start[i, k, x] for i in range(7)}
            total = None
            for i in range(7):
                if moving:
                    new[i, k, x] = values[i]
                total = values[i] if total is None else total + values[i]
            c12[k, (x - 1) * rows : x * rows, :] = total
            return carry

        lax.fori_loop(0, species, step, 0, unroll=4)
    react(rx, kc, c12, s12, w, rt)
    first = lax.axis_index("gy") == 0
    last = lax.axis_index("gy") == lax.axis_size("gy") - 1
    for x in range(planes):
        ux, uy, uz = u[0, x], u[1, x], u[2, x]
        if x in (0, planes - 1):
            cr, sr, half = c03, s03, slice((x > 0) * rows, (x > 0) * rows + rows)
        else:
            cr, sr, half = c12, s12, slice((x - 1) * rows, x * rows)

        def collide(k, carry, x=x, cr=cr, sr=sr, half=half, ux=ux, uy=uy, uz=uz):
            r = rk[k]
            keep = 1.0 - r
            a = r * cr[k, half, :]
            base = a + sr[k, half, :]
            base1 = 0.125 * base
            lean = 0.5 * a
            new[0, k, x] = keep * new[0, k, x] + 0.25 * base
            for i, v in ((1, ux), (3, uy), (5, uz)):
                d = lean * v
                up = keep * new[i, k, x] + (base1 + d)
                down = keep * new[i + 1, k, x] + (base1 - d)
                new[i, k, x] = up
                new[i + 1, k, x] = down
                if i == 3 and not moving:
                    spot = pl.ds(x * species + k, 1)
                    yu[spot, :] = jnp.where(last, 0.0, up[rows - 1 : rows])
                    yd[spot, :] = jnp.where(first, 0.0, down[0:1])
            return carry

        lax.fori_loop(0, species, collide, 0, unroll=4)


def flow_rows(q, x, post, hxu, hxd, species, part):
    planes = post.shape[1]
    src = x - VEL[q][0]
    if src < 0:
        return hxu[species + UPX.index(q), part, :]
    if src >= planes:
        return hxd[species + DNX.index(q), part, :]
    return post[q, src, part, :]


def flow_end_body(species, post, hxu, hxd, hyu, hyd, nt, out):
    planes, rows, lanes = post.shape[1:]
    base = species * planes
    at = row_index(rows, lanes)
    for x in range(planes):
        kind = nt[x]
        wall = kind == 1
        inlet = kind >= 2
        fuel = kind == 2
        for q in range(13, 27):
            moved = {}
            for p in {q, 26 - q}:
                a, b, c = VEL[p]
                value = flow_rows(p, x, post, hxu, hxd, species, slice(None))
                if b > 0:
                    spot = base + UPY.index(p) * planes + x
                    value = jnp.where(at == 0, hyu[spot : spot + 1, :], pltpu.roll(value, 1, 0))
                elif b < 0:
                    spot = base + DNY.index(p) * planes + x
                    value = jnp.where(
                        at == rows - 1, hyd[spot : spot + 1, :], pltpu.roll(value, rows - 1, 0)
                    )
                if c:
                    value = pltpu.roll(value, 1 if c > 0 else lanes - 1, 1)
                moved[p] = value
            for p in moved:
                cu = VEL[p][1] * SPEED
                fixed = [
                    WT[p] * (1.0 + 3.0 * s * cu + 4.5 * cu * cu - 1.5 * SPEED * SPEED)
                    for s in (1.0, -1.0)
                ]
                value = moved[p] if p == 13 else jnp.where(wall, moved[26 - p], moved[p])
                out[p, x] = jnp.where(inlet, jnp.where(fuel, fixed[0], fixed[1]), value)


def end_body(mode, *refs):
    refs = list(refs)
    g = refs.pop(0)
    hxu, hxd = [refs.pop(0) for _ in range(2)] if mode == 1 else (None, None)
    hyu, hyd = [refs.pop(0) for _ in range(2)] if mode == 3 else (None, None)
    nt, mix = [refs.pop(0) for _ in range(2)]
    if mode:
        refs.pop(0)
    out, buf, sem = refs
    species, planes = g.shape[1:3]
    inner = range(1, planes - 1)
    cover = {
        0: {0: range(planes), 5: range(planes), 1: inner},
        3: {3: range(planes)},
        1: {1: (0, planes - 1)},
    }[mode]
    chunk = 5 if species % 5 == 0 else species
    copies = []
    for start in range(0, species, chunk):
        for x in range(planes):
            pairs = [p for p, xs in cover.items() if x in xs]
            if not pairs:
                continue
            kind = nt[x]

            def step(k, carry, x=x, pairs=pairs, kind=kind):
                values = bounded(gather(k, x, g, hxu, hxd, hyu, hyd, pairs), kind, mix, k, species)
                for i, value in values.items():
                    buf[i - mode, k, x] = value
                return carry

            lax.fori_loop(start, start + chunk, step, 0, unroll=True)
        part = slice(start, start + chunk)
        for pair, xs in cover.items():
            for i in (0,) if pair == 0 else (pair, pair + 1):
                if pair != 1:
                    spans = [slice(0, planes)]
                elif mode == 0:
                    spans = [slice(1, planes - 1)]
                else:
                    spans = [slice(0, 1), slice(planes - 1, planes)]
                for span in spans:
                    copies.append(
                        pltpu.make_async_copy(
                            buf.at[i - mode, part, span], out.at[i, part, span], sem.at[len(copies)]
                        )
                    )
                    copies[-1].start()
    for copy in copies:
        copy.wait()


def per_device(populations, species, node_type, reactions, rate_const, species_rate, inlet_mix):
    planes, rows, lanes = node_type.shape
    count = species.shape[1]
    total = reactions.shape[0]
    pad = total % 2
    if pad:
        reactions = jnp.pad(reactions, ((0, pad), (0, 0)))
        rate_const = jnp.pad(rate_const, (0, pad))
        total += pad
    rx = reactions.T
    nt = inv(node_type)
    smem = [SM] * 4
    tables = (rx, rate_const, species_rate, inlet_mix)

    def arr(*shape):
        return VMEM(shape, F32)

    state = arr(7, count, planes, rows, lanes)
    inner = planes - 2
    edges = -(-2 * inner // 8) * 8
    wide = (2 * rows + edges) // 8
    react_out = arr(count, 2 * rows + edges, lanes)
    rates = VMEM((2 * total * 8, wide * lanes), BF16)
    rates_in = VMEM((2 * total * 8, inner * rows // 8 * lanes), BF16)
    inside = VMEM((count, inner * rows, lanes), F32)

    def swap(up, down, axis):
        size = lax.axis_size(axis)
        return lax.ppermute(up, axis, ring(size, 1)), lax.ppermute(down, axis, ring(size, -1))

    xmsg = arr(count + 9, rows, lanes)
    pv, sv, w, mu, md, c03, s03, fixed = call(
        first_body,
        "first",
        (hbm(populations), hbm(species), rx) + tables,
        [ANY, ANY, VM] + smem,
        (arr(27, planes, rows, lanes), state, VMEM((count * 8, 2 * total * 8), BF16), xmsg, xmsg,
         react_out, react_out, arr(3, count, lanes)),
        [VM] * 8,
        [rates, pltpu.SemaphoreType.DMA((planes,)), pltpu.SemaphoreType.DMA((planes,))],
    )
    hxu, hxd = swap(mu, md, "gx")
    u, post = call(
        flow_body,
        "flow",
        (inv(pv),),
        [VM],
        (arr(3, planes, rows, lanes), arr(27, planes, rows, lanes)),
        [VM] * 2,
    )
    g = None
    new = sv
    for s in range(SUBSTEPS):
        moving, flow = s > 0, s == 1
        ymsg = arr(count * planes + (9 * planes if flow else 0), lanes)
        if moving:
            xmsg = arr(count, rows, lanes)
            ins = [inv(v) for v in (g, hxu, hxd, hyu, hyd, node_type, u)]
            ins += list(tables) + [inv(w), inv(fixed)] + ([inv(post)] if flow else [])
            halo = hyu, hyd
            new, mu, md, yu, yd, c03, s03 = call(
                functools.partial(edge_body, flow),
                f"edge{s}",
                ins,
                [VM] * 7 + smem + [VM] * (3 if flow else 2),
                (state, xmsg, xmsg, ymsg, ymsg, react_out, react_out),
                [VM] * 7,
                [rates],
            )
            fhx = (hxu, hxd) if flow else fhx
            hxu, hxd = swap(mu, md, "gx")
            hyu, hyd = swap(yu, yd, "gy")
        ins = ([inv(g)] if moving else []) + [inv(v) for v in (new, c03, s03, u)]
        ins += list(tables[:3]) + [inv(w)]
        specs = [VM] * (5 if moving else 4) + smem[:3] + [VM]
        outs = (state,)
        if moving:
            ins += [inv(halo[0]), inv(halo[1]), nt, inlet_mix]
            specs += [VM, VM, VM, SM]
        else:
            outs += (ymsg, ymsg)
            fhx = None
        done = call(
            functools.partial(rest_body, moving),
            f"rest{s}",
            ins,
            specs,
            outs,
            [VM] * len(outs),
            [inside, inside, rates_in],
            alias={1 if moving else 0: 0},
        )
        g = done[0]
        if not moving:
            hyu, hyd = swap(done[1], done[2], "gy")
        if flow:
            fhy = hyu, hyd
    new_populations = call(
        functools.partial(flow_end_body, count),
        "flow_end",
        [inv(v) for v in (post,) + fhx + fhy] + [nt],
        [VM] * 6,
        jax.ShapeDtypeStruct((27, planes, rows, lanes), F32),
        VM,
    )
    result = None
    for mode, extra in ((0, ()), (3, (hyu, hyd)), (1, (hxu, hxd))):
        ins = [inv(v) for v in (g,) + extra] + [nt, inlet_mix] + ([hbm(result)] if mode else [])
        result = call(
            functools.partial(end_body, mode),
            f"end{mode}",
            ins,
            [VM] * (1 + len(extra)) + [VM, SM] + ([ANY] if mode else []),
            pltpu.HBM((7, count, planes, rows, lanes), F32),
            ANY,
            [VMEM((7 if mode == 0 else 2, count, planes, rows, lanes), F32),
             pltpu.SemaphoreType.DMA((32,))],
            alias={len(ins) - 1: 0} if mode else None,
        )
    return new_populations, result


def solution(mesh):
    flow = P(None, "gx", "gy", None)
    kinds = P(None, None, "gx", "gy", None)
    return jax.shard_map(
        per_device,
        mesh=mesh,
        in_specs=(flow, kinds, P("gx", "gy", None), P(), P(), P(), P()),
        out_specs=(flow, kinds),
        check_vma=False,
    )
```

```python
import functools

import jax
import jax.numpy as jnp
from jax import lax
from jax.experimental import pallas as pl
from jax.experimental.pallas import tpu as pltpu
from jax.sharding import PartitionSpec as P

SUBSTEPS = 3
CONC = 10
OMEGA = 1.6
SPEED = 0.05
F32 = jnp.float32
BF16 = jnp.bfloat16
VEL = [(a, b, c) for a in (-1, 0, 1) for b in (-1, 0, 1) for c in (-1, 0, 1)]
WT = [(8.0 / 27, 2.0 / 27, 1.0 / 54, 1.0 / 216)[abs(a) + abs(b) + abs(c)] for a, b, c in VEL]
UPX = [q for q in range(27) if VEL[q][0] > 0]
DNX = [q for q in range(27) if VEL[q][0] < 0]
UPY = [q for q in range(27) if VEL[q][1] > 0]
DNY = [q for q in range(27) if VEL[q][1] < 0]
MIB = 1 << 20
VMEM = pltpu.VMEM
VM = pl.BlockSpec(memory_space=pltpu.VMEM)
SM = pl.BlockSpec(memory_space=pltpu.SMEM)
ANY = pl.BlockSpec(memory_space=pl.ANY)


def inv(x):
    return pltpu.with_memory_space_constraint(x, pltpu.VMEM)


def hbm(x):
    return pltpu.with_memory_space_constraint(x, pltpu.HBM)


def ring(size, step):
    return [(i, (i + step) % size) for i in range(size)]


def call(body, name, ins, specs, outs, out_specs, scratch=(), alias=None, mib=12, cost=2_000_000):
    return pl.pallas_call(
        body,
        name=name,
        out_shape=outs,
        in_specs=specs,
        out_specs=out_specs,
        scratch_shapes=list(scratch),
        input_output_aliases=alias or {},
        compiler_params=pltpu.CompilerParams(vmem_limit_bytes=mib * MIB),
        cost_estimate=pl.CostEstimate(flops=cost, bytes_accessed=cost, transcendentals=0),
    )(*ins)


def react(rx, kc, c_ref, s_ref, w_ref, rt_ref, odd_ref=None, used=None):
    species, rows, lanes = c_ref.shape
    tiles = (used or rows) // 8
    half = rt_ref.shape[0] // 2
    even = tiles - tiles % 2
    for i in range(half // 16):
        rates = []
        for n in range(2):
            j = 2 * i + n
            rates.append(
                c_ref[rx[0, j], : 8 * tiles, :] * (c_ref[rx[1, j], : 8 * tiles, :] * kc[j])
            )
        for t in range(tiles):
            both = jnp.concatenate([r[8 * t : 8 * t + 8] for r in rates], axis=0)
            high = both.astype(BF16)
            low = (both - high.astype(F32)).astype(BF16)
            if t < even:
                rt_ref[16 * i : 16 * i + 16, lanes * t : lanes * (t + 1)] = high
                rt_ref[half + 16 * i : half + 16 * i + 16, lanes * t : lanes * (t + 1)] = low
            else:
                odd_ref[16 * i : 16 * i + 16, :lanes] = high
                odd_ref[16 * i : 16 * i + 16, lanes:] = low
    if even < tiles:
        total = jnp.dot(w_ref[:, :half], odd_ref[...], preferred_element_type=F32)
        total = total[:, :lanes] + total[:, lanes:]
        s_ref[:, 8 * even : 8 * tiles, :] = total.reshape(species, 8, lanes)
    total = jnp.dot(w_ref[...], rt_ref[:, : lanes * even], preferred_element_type=F32)
    for t in range(even):
        s_ref[:, 8 * t : 8 * t + 8, :] = total[:, lanes * t : lanes * (t + 1)].reshape(
            species, 8, lanes
        )


def moments(f):
    rho = f[0]
    for q in range(1, 27):
        rho = rho + f[q]
    parts = []
    for axis in range(3):
        plus = None
        for q in range(27):
            if VEL[q][axis] > 0:
                diff = f[q] - f[26 - q]
                plus = diff if plus is None else plus + diff
        parts.append(plus)
    scale = 1.0 / rho
    return rho, [p * scale for p in parts]


def cross(g, rk, c, s, ux, sign):
    a = rk * c
    return (1.0 - rk) * g + (0.125 * (a + s) + (0.5 * sign) * (a * ux))


def bands(species):
    return [(k, min(8, species - k)) for k in range(0, species, 8)]


def stoichiometry(rv, w):
    rows, width = w.shape
    half = width // 2
    species, total = rows // 8, half // 8

    def iota(shape, axis):
        return lax.broadcasted_iota(jnp.int32, shape, axis)

    def hot(test):
        return jnp.where(test, 1.0, 0.0)

    label = iota((species, total), 0)
    net = hot(rv[2:3, :] == label) - hot(rv[0:1, :] == label) - hot(rv[1:2, :] == label)
    tall = hot((iota((rows, species), 0) >> 3) == iota((rows, species), 1)).astype(BF16)
    wide = hot((iota((total, half), 1) >> 3) == iota((total, half), 0)).astype(BF16)
    part = jnp.dot(tall, net.astype(BF16), preferred_element_type=F32)
    full = jnp.dot(part.astype(BF16), wide, preferred_element_type=F32)
    same = (iota((rows, half), 0) & 7) == (iota((rows, half), 1) & 7)
    full = jnp.where(same, full, 0.0).astype(BF16)
    w[:, :half] = full
    w[:, half:] = full


def first_body(pop, spec, react_in, kc_in, rk_in, mix_in, pv, sv, w, mu, md, c03, s03, fixed,
               rx, kc, rk, mix, rt, rv, psem, ssem, tsem):
    planes, rows, lanes = pop.shape[1:]
    species = spec.shape[1]
    ends = (0, planes - 1)
    small = [
        pltpu.make_async_copy(src, dst, tsem.at[n])
        for n, (src, dst) in enumerate(
            ((react_in, rv), (react_in, rx), (kc_in, kc), (rk_in, rk), (mix_in, mix))
        )
    ]
    kinds = [pltpu.make_async_copy(spec.at[:, :, x], sv.at[:, :, x], ssem.at[n])
             for n, x in enumerate(ends)]
    flows = [pltpu.make_async_copy(pop.at[:, x], pv.at[:, x], psem.at[n])
             for n, x in enumerate(ends)]
    for copy in small + kinds + flows:
        copy.start()
    height = c03.shape[1]
    if height > 2 * rows:
        for k in range(species):
            c03[k, 2 * rows :, :] = jnp.zeros((height - 2 * rows, lanes), F32)
    for copy in small:
        copy.wait()
    stoichiometry(rv, w)
    for k in range(species):
        for n, value in enumerate((rk[k], mix[0, k], mix[1, k])):
            fixed[n, k : k + 1, :] = jnp.full((1, lanes), value, F32)
    for side in range(2):
        for n, i in enumerate((0, 1, 3, 4)):
            fixed[3 + 4 * side + n] = inlet_weight(i, side) * fixed[1 + side]
    for n, x in enumerate(ends):
        kinds[n].wait()

        def conc(k, carry, n=n, x=x):
            total = sv[0, k, x]
            for i in range(1, 7):
                total = total + sv[i, k, x]
            c03[k, n * rows : (n + 1) * rows, :] = total
            return carry

        lax.fori_loop(0, species, conc, 0, unroll=5)
    react(rx, kc, c03, s03, w, rt, used=2 * rows)
    for n, x in enumerate(ends):
        flows[n].wait()
        f = [pv[q, x] for q in range(27)]
        rho, v = moments(f)
        ux = v[0]
        out, i, sign = ((md, 2, -1.0), (mu, 1, 1.0))[n]

        def send(k, carry, n=n, x=x, out=out, i=i, sign=sign, ux=ux):
            half = slice(n * rows, (n + 1) * rows)
            out[k] = cross(sv[i, k, x], rk[k], c03[k, half, :], s03[k, half, :], ux, sign)
            return carry

        lax.fori_loop(0, species, send, 0, unroll=5)
        for m, q in enumerate((DNX, UPX)[n]):
            still, scaled, (even, odd) = relaxed(rho, v, q)
            out[species + m] = (1.0 - OMEGA) * f[q] + WT[q] * scaled * (even + odd)


def relaxed(rho, v, q):
    still = 1.0 - 1.5 * (v[0] * v[0] + v[1] * v[1] + v[2] * v[2])
    along = None
    for axis in range(3):
        if VEL[q][axis]:
            term = v[axis] if VEL[q][axis] > 0 else -v[axis]
            along = term if along is None else along + term
    return still, OMEGA * rho, (still + 4.5 * along * along, 3.0 * along)


def flow_body(pop, spec, pv_in, sv_in, pv, sv, u, post, psem, ssem):
    del pv_in, sv_in
    planes = pv.shape[1]
    inner = range(1, planes - 1)
    flows = [pltpu.make_async_copy(pop.at[:, x], pv.at[:, x], psem.at[x]) for x in inner]
    kinds = [pltpu.make_async_copy(spec.at[:, :, x], sv.at[:, :, x], ssem.at[x]) for x in inner]
    for copy in flows + kinds:
        copy.start()
    for x in [0, planes - 1] + list(inner):
        if x in inner:
            flows[x - 1].wait()
        f = [pv[q, x] for q in range(27)]
        rho, v = moments(f)
        for axis in range(3):
            u[axis, x] = v[axis]
        for q in range(14, 27):
            still, scaled, (even, odd) = relaxed(rho, v, q)
            ws = WT[q] * scaled
            for p, value in ((q, even + odd), (26 - q, even - odd)):
                post[p, x] = (1.0 - OMEGA) * f[p] + ws * value
        post[13, x] = (1.0 - OMEGA) * f[13] + WT[13] * scaled * still
    for copy in kinds:
        copy.wait()


def row_index(rows, lanes):
    return lax.broadcasted_iota(jnp.int32, (rows, lanes), 0)


def gather(k, x, g, hxu, hxd, hyu, hyd, pairs):
    species, planes, rows, lanes = g.shape[1:]
    out = {}
    if 0 in pairs:
        out[0] = g[0, k, x]
    if 1 in pairs:
        out[1] = g[1, k, x - 1] if x > 0 else hxu[k]
        out[2] = g[2, k, x + 1] if x < planes - 1 else hxd[k]
    if 3 in pairs:
        flat = g.reshape(7 * species * planes * rows, lanes)
        at = row_index(8, lanes)
        spot = pl.ds(x * species + k, 1)
        for i, step, halo in ((3, -1, hyu), (4, 1, hyd)):
            base = ((i * species + k) * planes + x) * rows + step
            parts = [flat[pl.ds(base + t, 8), :] for t in range(0, rows, 8)]
            edge, row = (0, 0) if step < 0 else (-1, 7)
            parts[edge] = jnp.where(at == row, halo[spot, :], parts[edge])
            out[i] = jnp.concatenate(parts, axis=0)
    if 5 in pairs:
        out[5] = pltpu.roll(g[5, k, x], 1, 1)
        out[6] = pltpu.roll(g[6, k, x], lanes - 1, 1)
    return out


def masks(nt, x):
    rows = nt.shape[1]
    return nt[x] == 1, nt[x, :8, :] == 2, nt[x, rows - 8 :, :] == 3


def settle(value, kind, k, fixed, base):
    _, low, high = kind
    spot = pl.ds(k, 1)
    first = jnp.where(low, fixed[base[0], spot, :], value[:8])
    if value.shape[0] == 8:
        return jnp.where(high, fixed[base[1], spot, :], first)
    last = jnp.where(high, fixed[base[1], spot, :], value[-8:])
    return jnp.concatenate([first, value[8:-8], last] if value.shape[0] > 16 else [first, last], 0)


def walled(moved, kind, k, fixed):
    swap = (0, 2, 1, 4, 3, 6, 5)
    out = {}
    for i, m in moved.items():
        n = {0: 0, 3: 2, 4: 3}.get(i, 1)
        value = m if i == 0 else jnp.where(kind[0], moved[swap[i]], m)
        out[i] = settle(value, kind, k, fixed, (3 + n, 7 + n))
    return out


def inlet_weight(i, side):
    tilt = 4.0 * SPEED * (1.0 if side == 0 else -1.0)
    return {0: 0.25, 3: 0.125 * (1.0 + tilt), 4: 0.125 * (1.0 - tilt)}.get(i, 0.125)


def edge_body(flow, *refs):
    refs = list(refs)
    g, hxu, hxd, hyu, hyd, nt, u, rx, kc, rk, w, fixed = [refs.pop(0) for _ in range(12)]
    post = refs.pop(0) if flow else None
    if not flow:
        refs.pop(0)
    new, mu, md, yu, yd, c03, s03, rt, odd = refs
    species, planes, rows, lanes = g.shape[1:]
    height = c03.shape[1]
    ends = (0, planes - 1)
    flat = g.reshape(7 * species * planes * rows, lanes)
    fresh = new.reshape(7 * species * planes * rows, lanes)
    cflat = c03.reshape(species * height, lanes)
    sflat = s03.reshape(species * height, lanes)
    jump = planes * rows
    zeros = height - 2 * rows
    for k in range(species):
        c03[k, 2 * rows :, :] = jnp.zeros((zeros, lanes), F32)
    for x in range(1, planes - 1):
        for side, row in ((0, 0), (1, rows - 1)):
            kind = nt[x, row : row + 1, :]
            for k, size in bands(species):

                def load(i, plane, r, k=k, size=size):
                    return flat[pl.ds(((i * species + k) * planes + plane) * rows + r, size, jump), :]

                halo = slice(x * species + k, x * species + k + size)
                moved = {
                    0: load(0, x, row),
                    1: load(1, x - 1, row),
                    2: load(2, x + 1, row),
                    3: hyu[halo, :] if side == 0 else load(3, x, row - 1),
                    4: hyd[halo, :] if side == 1 else load(4, x, row + 1),
                    5: pltpu.roll(load(5, x, row), 1, 1),
                    6: pltpu.roll(load(6, x, row), lanes - 1, 1),
                }
                wide = jnp.broadcast_to(kind, (size, lanes))
                inlet = wide == 2 + side
                value = fixed[1 + side, k : k + size, :]
                total = moved[0]
                for i in range(1, 7):
                    total = total + moved[i]
                total = jnp.where(inlet, value, total)
                i = 3 if side else 4
                kept = jnp.where(wide == 1, moved[7 - i], moved[i])
                kept = jnp.where(inlet, inlet_weight(i, side) * value, kept)
                spot = 2 * rows + 2 * (x - 1) + side
                cflat[pl.ds(k * height + spot, size, height), :] = total
                (yu if side else yd)[halo, :] = kept
    for n, x in enumerate(ends):
        kind = masks(nt, x)

        def step(k, carry, n=n, x=x, kind=kind):
            moved = gather(k, x, g, hxu, hxd, hyu, hyd, (0, 1, 3, 5))
            values = walled(moved, kind, k, fixed)
            total = moved[0]
            for i in range(1, 7):
                total = total + moved[i]
            for i in range(7):
                new[i, k, x] = values[i]
            c03[k, n * rows : (n + 1) * rows, :] = settle(total, kind, k, fixed, (1, 2))
            return carry

        lax.fori_loop(0, species, step, 0, unroll=CONC)
    react(rx, kc, c03, s03, w, rt, odd)
    for n, x in enumerate(ends):
        ux = u[0, x]
        out, i, sign = ((md, 2, -1.0), (mu, 1, 1.0))[n]

        def send(k, carry, n=n, x=x, out=out, i=i, sign=sign, ux=ux):
            half = slice(n * rows, (n + 1) * rows)
            out[k] = cross(new[i, k, x], rk[k], c03[k, half, :], s03[k, half, :], ux, sign)
            return carry

        lax.fori_loop(0, species, send, 0, unroll=5)
    first = lax.axis_index("gy") == 0
    last = lax.axis_index("gy") == lax.axis_size("gy") - 1
    for x in range(planes):
        for side, row in ((0, 0), (1, rows - 1)):
            uy = u[1, x, row : row + 1, :]
            out, i, sign, off = ((yd, 4, -1.0, first), (yu, 3, 1.0, last))[side]
            if x in ends:
                spot = (x > 0) * rows + row
            else:
                spot = 2 * rows + 2 * (x - 1) + side
            for k, size in bands(species):
                halo = slice(x * species + k, x * species + k + size)
                if x in ends:
                    at = ((i * species + k) * planes + x) * rows + row
                    value = fresh[pl.ds(at, size, jump), :]
                else:
                    value = out[halo, :]
                c = cflat[pl.ds(k * height + spot, size, height), :]
                s = sflat[pl.ds(k * height + spot, size, height), :]
                value = cross(value, fixed[0, k : k + size, :], c, s, uy, sign)
                out[halo, :] = jnp.where(off, 0.0, value)
    if flow:
        base = species * planes
        for out, queue, row, off in ((yu, UPY, rows - 1, last), (yd, DNY, 0, first)):
            for n, q in enumerate(queue):
                for x in range(planes):
                    at = base + n * planes + x
                    value = flow_rows(q, x, post, hxu, hxd, species, slice(row, row + 1))
                    out[at : at + 1, :] = jnp.where(off, 0.0, value)


def rest_body(moving, *refs):
    refs = list(refs)
    g = refs.pop(0) if moving else None
    start, c03, s03, u, rx, kc, rk, w = [refs.pop(0) for _ in range(8)]
    if moving:
        hyu, hyd, nt, fixed = [refs.pop(0) for _ in range(4)]
    new = refs.pop(0)
    if not moving:
        yu, yd = [refs.pop(0) for _ in range(2)]
    c12, s12, rt = refs
    species, planes, rows, lanes = new.shape[1:]
    for x in range(1, planes - 1):
        kind = masks(nt, x) if moving else None

        def step(k, carry, x=x, kind=kind):
            if moving:
                moved = gather(k, x, g, None, None, hyu, hyd, (0, 1, 3, 5))
                values = walled(moved, kind, k, fixed)
            else:
                moved = {i: start[i, k, x] for i in range(7)}
            total = moved[0]
            for i in range(1, 7):
                total = total + moved[i]
            if moving:
                for i in range(7):
                    new[i, k, x] = values[i]
                total = settle(total, kind, k, fixed, (1, 2))
            c12[k, (x - 1) * rows : x * rows, :] = total
            return carry

        lax.fori_loop(0, species, step, 0, unroll=CONC)
    react(rx, kc, c12, s12, w, rt)
    first = lax.axis_index("gy") == 0
    last = lax.axis_index("gy") == lax.axis_size("gy") - 1
    for x in range(planes):
        ux, uy, uz = 0.5 * u[0, x], 0.5 * u[1, x], 0.5 * u[2, x]
        if x in (0, planes - 1):
            cr, sr, half = c03, s03, slice((x > 0) * rows, (x > 0) * rows + rows)
        else:
            cr, sr, half = c12, s12, slice((x - 1) * rows, x * rows)

        def collide(k, carry, x=x, cr=cr, sr=sr, half=half, ux=ux, uy=uy, uz=uz):
            r = rk[k]
            keep = 1.0 - r
            a = r * cr[k, half, :]
            base1 = 0.125 * (a + sr[k, half, :])
            new[0, k, x] = keep * new[0, k, x] + (base1 + base1)
            for i, v in ((1, ux), (3, uy), (5, uz)):
                d = a * v
                up = keep * new[i, k, x] + (base1 + d)
                down = keep * new[i + 1, k, x] + (base1 - d)
                new[i, k, x] = up
                new[i + 1, k, x] = down
                if i == 3 and not moving:
                    spot = pl.ds(x * species + k, 1)
                    yu[spot, :] = jnp.where(last, 0.0, up[rows - 1 : rows])
                    yd[spot, :] = jnp.where(first, 0.0, down[0:1])
            return carry

        lax.fori_loop(0, species, collide, 0, unroll=5)


def flow_rows(q, x, post, hxu, hxd, species, part):
    planes = post.shape[1]
    src = x - VEL[q][0]
    if src < 0:
        return hxu[species + UPX.index(q), part, :]
    if src >= planes:
        return hxd[species + DNX.index(q), part, :]
    return post[q, src, part, :]


def flow_end_body(species, post, hxu, hxd, hyu, hyd, nt, result, token, out, sem):
    planes, rows, lanes = post.shape[1:]
    base = species * planes
    token[...] = jnp.zeros(token.shape, F32)
    copies = []
    at = row_index(rows, lanes)
    for x in range(planes):
        kind = nt[x]
        wall = kind == 1
        inlet = kind >= 2
        fuel = kind == 2
        for q in range(13, 27):
            moved = {}
            for p in {q, 26 - q}:
                a, b, c = VEL[p]
                value = flow_rows(p, x, post, hxu, hxd, species, slice(None))
                if b > 0:
                    spot = base + UPY.index(p) * planes + x
                    value = jnp.where(at == 0, hyu[spot : spot + 1, :], pltpu.roll(value, 1, 0))
                elif b < 0:
                    spot = base + DNY.index(p) * planes + x
                    value = jnp.where(
                        at == rows - 1, hyd[spot : spot + 1, :], pltpu.roll(value, rows - 1, 0)
                    )
                if c:
                    value = pltpu.roll(value, 1 if c > 0 else lanes - 1, 1)
                moved[p] = value
            for p in moved:
                cu = VEL[p][1] * SPEED
                fixed = [
                    WT[p] * (1.0 + 3.0 * s * cu + 4.5 * cu * cu - 1.5 * SPEED * SPEED)
                    for s in (1.0, -1.0)
                ]
                value = moved[p] if p == 13 else jnp.where(wall, moved[26 - p], moved[p])
                out[p, x] = jnp.where(inlet, jnp.where(fuel, fixed[0], fixed[1]), value)
        copies.append(pltpu.make_async_copy(out.at[:, x], result.at[:, x], sem.at[x]))
        copies[-1].start()
    for copy in copies:
        copy.wait()


def end_body(mode, *refs):
    refs = list(refs)
    g = refs.pop(0)
    hxu, hxd = [refs.pop(0) for _ in range(2)] if mode == 1 else (None, None)
    hyu, hyd = [refs.pop(0) for _ in range(2)] if mode == 3 else (None, None)
    nt, fixed = [refs.pop(0) for _ in range(2)]
    if mode:
        refs.pop(0)
    out, buf, sem = refs
    species, planes = g.shape[1:3]
    inner = range(1, planes - 1)
    cover = {
        0: {0: range(planes), 5: range(planes), 1: inner},
        3: {3: range(planes)},
        1: {1: (0, planes - 1)},
    }[mode]
    chunk = 5 if species % 5 == 0 else 1
    copies = []
    for start in range(0, species, chunk):
        for x in range(planes):
            pairs = [p for p, xs in cover.items() if x in xs]
            if not pairs:
                continue
            kind = masks(nt, x)

            def step(k, carry, x=x, pairs=pairs, kind=kind):
                values = walled(gather(k, x, g, hxu, hxd, hyu, hyd, pairs), kind, k, fixed)
                for i, value in values.items():
                    buf[i - mode, k, x] = value
                return carry

            lax.fori_loop(start, start + chunk, step, 0, unroll=True)
        part = slice(start, start + chunk)
        for pair, xs in cover.items():
            for i in (0,) if pair == 0 else (pair, pair + 1):
                if pair != 1:
                    spans = [slice(0, planes)]
                elif mode == 0:
                    spans = [slice(1, planes - 1)]
                else:
                    spans = [slice(0, 1), slice(planes - 1, planes)]
                for span in spans:
                    copies.append(
                        pltpu.make_async_copy(
                            buf.at[i - mode, part, span], out.at[i, part, span], sem.at[len(copies)]
                        )
                    )
                    copies[-1].start()
    for copy in copies:
        copy.wait()


def per_device(populations, species, node_type, reactions, rate_const, species_rate, inlet_mix):
    planes, rows, lanes = node_type.shape
    count = species.shape[1]
    total = reactions.shape[0]
    pad = total % 2
    if pad:
        reactions = jnp.pad(reactions, ((0, pad), (0, 0)))
        rate_const = jnp.pad(rate_const, (0, pad))
        total += pad
    nt = inv(node_type)
    smem = [SM] * 3

    def arr(*shape):
        return VMEM(shape, F32)

    state = arr(7, count, planes, rows, lanes)
    inner = planes - 2
    edges = -(-2 * inner // 8) * 8
    wide = (2 * rows + edges) // 8
    react_out = arr(count, 2 * rows + edges, lanes)
    rates = VMEM((2 * total * 8, wide // 2 * 2 * lanes), BF16)
    odd = VMEM((total * 8, 2 * lanes), BF16)
    rates_in = VMEM((2 * total * 8, inner * rows // 8 * lanes), BF16)
    inside = VMEM((count, inner * rows, lanes), F32)

    def swap(up, down, axis):
        size = lax.axis_size(axis)
        return lax.ppermute(up, axis, ring(size, 1)), lax.ppermute(down, axis, ring(size, -1))

    xmsg = arr(count + 9, rows, lanes)
    sems = [pltpu.SemaphoreType.DMA((planes,)), pltpu.SemaphoreType.DMA((planes,))]
    ints = pltpu.SMEM((3, total), jnp.int32)
    flows = arr(27, planes, rows, lanes)
    pv, sv, w, mu, md, c03, s03, fixed, *tables = call(
        first_body,
        "first",
        [hbm(v) for v in (populations, species, reactions.T, rate_const, species_rate, inlet_mix)],
        [ANY] * 6,
        (flows, state, VMEM((count * 8, 2 * total * 8), BF16), xmsg, xmsg, react_out, react_out,
         arr(11, count, lanes), ints, pltpu.SMEM((total,), F32), pltpu.SMEM((count,), F32)),
        [VM] * 8 + [SM] * 3,
        [pltpu.SMEM((2, count), F32), rates, VMEM((3, total), jnp.int32)] + sems
        + [pltpu.SemaphoreType.DMA((5,))],
    )
    tables = [pltpu.with_memory_space_constraint(v, pltpu.SMEM) for v in tables]
    hxu, hxd = swap(mu, md, "gx")
    pv, sv, u, post = call(
        flow_body,
        "flow",
        (hbm(populations), hbm(species), inv(pv), inv(sv)),
        [ANY, ANY, VM, VM],
        (flows, state, arr(3, planes, rows, lanes), flows),
        [VM] * 4,
        sems,
        alias={2: 0, 3: 1},
    )
    g = None
    new = sv
    for s in range(SUBSTEPS):
        moving, flow = s > 0, s == 1
        ymsg = arr(count * planes + (9 * planes if flow else 0), lanes)
        if moving:
            xmsg = arr(count, rows, lanes)
            ins = [inv(v) for v in (g, hxu, hxd, hyu, hyd, node_type, u)]
            ins += list(tables) + [inv(w), inv(fixed), inv(post if flow else token)]
            halo = hyu, hyd
            new, mu, md, yu, yd, c03, s03 = call(
                functools.partial(edge_body, flow),
                f"edge{s}",
                ins,
                [VM] * 7 + smem + [VM] * 3,
                (state, xmsg, xmsg, ymsg, ymsg, react_out, react_out),
                [VM] * 7,
                [rates, odd],
            )
            fhx = (hxu, hxd) if flow else fhx
            hxu, hxd = swap(mu, md, "gx")
            hyu, hyd = swap(yu, yd, "gy")
        ins = ([inv(g)] if moving else []) + [inv(v) for v in (new, c03, s03, u)]
        ins += list(tables) + [inv(w)]
        specs = [VM] * (5 if moving else 4) + smem + [VM]
        outs = (state,)
        if moving:
            ins += [inv(halo[0]), inv(halo[1]), nt, inv(fixed)]
            specs += [VM] * 4
        else:
            outs += (ymsg, ymsg)
            fhx = None
        done = call(
            functools.partial(rest_body, moving),
            f"rest{s}",
            ins,
            specs,
            outs,
            [VM] * len(outs),
            [inside, inside, rates_in],
            alias={1 if moving else 0: 0},
        )
        g = done[0]
        if not moving:
            hyu, hyd = swap(done[1], done[2], "gy")
        if flow:
            fhy = hyu, hyd
            new_populations, token = call(
                functools.partial(flow_end_body, count),
                "flow_end",
                [inv(v) for v in (post,) + fhx + fhy] + [nt],
                [VM] * 6,
                (pltpu.HBM((27, planes, rows, lanes), F32), arr(8, lanes)),
                [ANY, VM],
                [flows, sems[0]],
            )
    result = None
    for mode, extra in ((0, ()), (3, (hyu, hyd)), (1, (hxu, hxd))):
        ins = [inv(v) for v in (g,) + extra] + [nt, inv(fixed)] + ([hbm(result)] if mode else [])
        result = call(
            functools.partial(end_body, mode),
            f"end{mode}",
            ins,
            [VM] * (3 + len(extra)) + ([ANY] if mode else []),
            pltpu.HBM((7, count, planes, rows, lanes), F32),
            ANY,
            [VMEM((7 if mode == 0 else 2, count, planes, rows, lanes), F32),
             pltpu.SemaphoreType.DMA((32,))],
            alias={len(ins) - 1: 0} if mode else None,
        )
    return new_populations, result


def solution(mesh):
    flow = P(None, "gx", "gy", None)
    kinds = P(None, None, "gx", "gy", None)
    return jax.shard_map(
        per_device,
        mesh=mesh,
        in_specs=(flow, kinds, P("gx", "gy", None), P(), P(), P(), P()),
        out_specs=(flow, kinds),
        check_vma=False,
    )
```

```python
import functools

import jax
import jax.numpy as jnp
from jax import lax
from jax.experimental import pallas as pl
from jax.experimental.pallas import tpu as pltpu
from jax.sharding import PartitionSpec as P


SUBSTEPS = 3
CONC = 10
OMEGA = 1.6
SPEED = 0.05
F32 = jnp.float32
BF16 = jnp.bfloat16
VEL = [(a, b, c) for a in (-1, 0, 1) for b in (-1, 0, 1) for c in (-1, 0, 1)]
WT = [(8.0 / 27, 2.0 / 27, 1.0 / 54, 1.0 / 216)[abs(a) + abs(b) + abs(c)] for a, b, c in VEL]
UPX = [q for q in range(27) if VEL[q][0] > 0]
DNX = [q for q in range(27) if VEL[q][0] < 0]
UPY = [q for q in range(27) if VEL[q][1] > 0]
DNY = [q for q in range(27) if VEL[q][1] < 0]
MIB = 1 << 20
VMEM = pltpu.VMEM
VM = pl.BlockSpec(memory_space=pltpu.VMEM)
SM = pl.BlockSpec(memory_space=pltpu.SMEM)
ANY = pl.BlockSpec(memory_space=pl.ANY)


def inv(x):
    return pltpu.with_memory_space_constraint(x, pltpu.VMEM)


def hbm(x):
    return pltpu.with_memory_space_constraint(x, pltpu.HBM)


def pairs(size, near):
    if near:
        return [(i, i ^ 1) for i in range(size)]
    return [(i, (i + 1 if i % 2 else i - 1) % size) for i in range(size)]


def is_even(axis):
    return lax.rem(lax.axis_index(axis), 2) == 0


def pick(even, one, other):
    return jnp.where(even, one, other)


class Halo:
    def __init__(self, near, far, axis):
        self.near, self.far, self.even = near, far, is_even(axis)

    def up(self, *at):
        return pick(self.even, self.far[at], self.near[at])

    def down(self, *at):
        return pick(self.even, self.near[at], self.far[at])


def call(body, ins, specs, outs, out_specs, scratch=(), alias=None, mib=12, cost=2_000_000):
    return pl.pallas_call(
        body,
        out_shape=outs,
        in_specs=specs,
        out_specs=out_specs,
        scratch_shapes=list(scratch),
        input_output_aliases=alias or {},
        compiler_params=pltpu.CompilerParams(vmem_limit_bytes=mib * MIB),
        cost_estimate=pl.CostEstimate(flops=cost, bytes_accessed=cost, transcendentals=0),
    )(*ins)


def react(rx, kc, c_ref, s_ref, w_ref, rt_ref, odd_ref=None, start=0, stop=None):
    species, rows, lanes = c_ref.shape
    part = slice(start, stop or rows)
    tiles = (part.stop - part.start) // 8
    half = w_ref.shape[1] // 2
    even = tiles - tiles % 2
    for i in range(half // 16):
        rates = []
        for n in range(2):
            j = 2 * i + n
            rates.append(c_ref[rx[0, j], part, :] * (c_ref[rx[1, j], part, :] * kc[j]))
        for t in range(tiles):
            both = jnp.concatenate([r[8 * t : 8 * t + 8] for r in rates], axis=0)
            high = both.astype(BF16)
            low = (both - high.astype(F32)).astype(BF16)
            if t < even:
                rt_ref[16 * i : 16 * i + 16, lanes * t : lanes * (t + 1)] = high
                rt_ref[half + 16 * i : half + 16 * i + 16, lanes * t : lanes * (t + 1)] = low
            else:
                odd_ref[16 * i : 16 * i + 16, :lanes] = high
                odd_ref[16 * i : 16 * i + 16, lanes:] = low
    if even < tiles:
        total = jnp.dot(w_ref[:, :half], odd_ref[...], preferred_element_type=F32)
        total = total[:, :lanes] + total[:, lanes:]
        s_ref[:, start + 8 * even : start + 8 * tiles, :] = total.reshape(species, 8, lanes)
    if even:
        total = jnp.dot(w_ref[...], rt_ref[:, : lanes * even], preferred_element_type=F32)
        for t in range(even):
            s_ref[:, start + 8 * t : start + 8 * t + 8, :] = total[
                :, lanes * t : lanes * (t + 1)
            ].reshape(species, 8, lanes)


def moments(f):
    rho = f[0]
    for q in range(1, 27):
        rho = rho + f[q]
    parts = []
    for axis in range(3):
        plus = None
        for q in range(27):
            if VEL[q][axis] > 0:
                diff = f[q] - f[26 - q]
                plus = diff if plus is None else plus + diff
        parts.append(plus)
    scale = 1.0 / rho
    return rho, [p * scale for p in parts]


def cross(g, rk, c, s, ux, sign):
    a = rk * c
    return (1.0 - rk) * g + (0.125 * (a + s) + (0.5 * sign) * (a * ux))


def bands(species):
    return [(k, min(8, species - k)) for k in range(0, species, 8)]


def stoichiometry(rv, w):
    rows, width = w.shape
    half = width // 2
    species, total = rows // 8, half // 8

    def iota(shape, axis):
        return lax.broadcasted_iota(jnp.int32, shape, axis)

    def hot(test):
        return jnp.where(test, 1.0, 0.0)

    label = iota((species, total), 0)
    net = hot(rv[2:3, :] == label) - hot(rv[0:1, :] == label) - hot(rv[1:2, :] == label)
    tall = hot((iota((rows, species), 0) >> 3) == iota((rows, species), 1)).astype(BF16)
    wide = hot((iota((total, half), 1) >> 3) == iota((total, half), 0)).astype(BF16)
    part = jnp.dot(tall, net.astype(BF16), preferred_element_type=F32)
    full = jnp.dot(part.astype(BF16), wide, preferred_element_type=F32)
    same = (iota((rows, half), 0) & 7) == (iota((rows, half), 1) & 7)
    full = jnp.where(same, full, 0.0).astype(BF16)
    w[:, :half] = full
    w[:, half:] = full


def first_body(pop, spec, react_in, kc_in, rk_in, mix_in, sv, w, ma, mb, ya, yb, c03, s03,
               fixed, u, post, rx, kc, rk, mix, rt, odd, keep, rv, psem, ssem, tsem, pv):
    planes, rows, lanes = pop.shape[1:]
    species = spec.shape[1]
    ends = (0, planes - 1)
    inner = range(1, planes - 1)
    small = [
        pltpu.make_async_copy(src, dst, tsem.at[n])
        for n, (src, dst) in enumerate(
            ((react_in, rv), (react_in, rx), (kc_in, kc), (rk_in, rk), (mix_in, mix))
        )
    ]
    kinds = [pltpu.make_async_copy(spec.at[:, :, x], sv.at[:, :, x], ssem.at[x])
             for x in range(planes)]
    flows = [pltpu.make_async_copy(pop.at[:, x], pv.at[:, x], psem.at[x]) for x in range(planes)]
    for copy in small + [kinds[x] for x in ends] + flows + [kinds[x] for x in inner]:
        copy.start()
    for k in range(species):
        c03[k, 2 * rows :, :] = jnp.zeros((c03.shape[1] - 2 * rows, lanes), F32)
    for copy in small:
        copy.wait()
    stoichiometry(rv, w)
    for k in range(species):
        for n, value in enumerate((rk[k], mix[0, k], mix[1, k])):
            fixed[n, k : k + 1, :] = jnp.full((1, lanes), value, F32)
    for side in range(2):
        for n, i in enumerate((0, 1, 3, 4)):
            fixed[3 + 4 * side + n] = inlet_weight(i, side) * fixed[1 + side]
    for n, x in enumerate(ends):
        kinds[x].wait()

        def conc(k, carry, n=n, x=x):
            total = sv[0, k, x]
            for i in range(1, 7):
                total = total + sv[i, k, x]
            c03[k, n * rows : (n + 1) * rows, :] = total
            return carry

        lax.fori_loop(0, species, conc, 0, unroll=5)
    react(rx, kc, c03, s03, w, rt, start=0, stop=2 * rows)
    for copy in flows:
        copy.wait()
    collide_flow(pv, u, post)
    for x in inner:
        kinds[x].wait()
    flat = sv.reshape(7 * species * planes * rows, lanes)
    height = c03.shape[1]
    cflat = c03.reshape(species * height, lanes)
    for x in inner:
        for side, row in ((0, 0), (1, rows - 1)):
            for k, size in bands(species):
                values = [
                    flat[pl.ds(((i * species + k) * planes + x) * rows + row, size, planes * rows), :]
                    for i in range(7)
                ]
                total = values[0]
                for i in range(1, 7):
                    total = total + values[i]
                spot = 2 * rows + 2 * (x - 1) + side
                cflat[pl.ds(k * height + spot, size, height), :] = total
                keep[side, x * species + k : x * species + k + size, :] = values[3 if side else 4]
    react(rx, kc, c03, s03, w, rt, odd, start=2 * rows)
    send_faces(sv, rk, c03, s03, [u[0, x] for x in ends], ma, mb)
    send_rows(sv, keep, c03, s03, fixed, u, ya, yb)
    first, last, even = edge_flags()
    for n in range(9):
        for x in range(planes):
            at = slice((species + n) * planes + x, (species + n) * planes + x + 1)
            top = jnp.where(last, 0.0, post[UPY[n], x, rows - 1 : rows, :])
            bottom = jnp.where(first, 0.0, post[DNY[n], x, 0:1, :])
            ya[at, :] = pick(even, top, bottom)
            yb[at, :] = pick(even, bottom, top)


def edge_flags():
    rank, size = lax.axis_index("gy"), lax.axis_size("gy")
    return rank == 0, rank == size - 1, is_even("gy")


def send_rows(state, keep, c03, s03, fixed, u, ya, yb):
    species, planes, rows, lanes = state.shape[1:]
    height = c03.shape[1]
    fresh = state.reshape(7 * species * planes * rows, lanes)
    cflat = c03.reshape(species * height, lanes)
    sflat = s03.reshape(species * height, lanes)
    first, last, even = edge_flags()
    for x in range(planes):
        for k, size in bands(species):
            halo = slice(x * species + k, x * species + k + size)
            sent = []
            for side, row, off in ((0, 0, first), (1, rows - 1, last)):
                i, sign = (3, 1.0) if side else (4, -1.0)
                if x in (0, planes - 1):
                    spot = (x > 0) * rows + row
                    at = ((i * species + k) * planes + x) * rows + row
                    value = fresh[pl.ds(at, size, planes * rows), :]
                else:
                    spot = 2 * rows + 2 * (x - 1) + side
                    value = keep[side, halo, :]
                c = cflat[pl.ds(k * height + spot, size, height), :]
                s = sflat[pl.ds(k * height + spot, size, height), :]
                uy = u[1, x, row : row + 1, :]
                value = cross(value, fixed[0, k : k + size, :], c, s, uy, sign)
                sent.append(jnp.where(off, 0.0, value))
            ya[halo, :] = pick(even, sent[1], sent[0])
            yb[halo, :] = pick(even, sent[0], sent[1])


def send_faces(state, rk, c03, s03, speeds, ma, mb):
    species, planes, rows = state.shape[1:4]
    even = is_even("gx")

    def send(k, carry):
        low = cross(state[2, k, 0], rk[k], c03[k, :rows, :], s03[k, :rows, :], speeds[0], -1.0)
        part = slice(rows, 2 * rows)
        high = cross(
            state[1, k, planes - 1], rk[k], c03[k, part, :], s03[k, part, :], speeds[1], 1.0
        )
        ma[k] = pick(even, high, low)
        mb[k] = pick(even, low, high)
        return carry

    lax.fori_loop(0, species, send, 0, unroll=5)


def relaxed(rho, v, q):
    still = 1.0 - 1.5 * (v[0] * v[0] + v[1] * v[1] + v[2] * v[2])
    along = None
    for axis in range(3):
        if VEL[q][axis]:
            term = v[axis] if VEL[q][axis] > 0 else -v[axis]
            along = term if along is None else along + term
    return still, OMEGA * rho, (still + 4.5 * along * along, 3.0 * along)


def collide_flow(pv, u, post):
    for x in range(pv.shape[1]):
        f = [pv[q, x] for q in range(27)]
        rho, v = moments(f)
        for axis in range(3):
            u[axis, x] = v[axis]
        for q in range(14, 27):
            still, scaled, (even, odd) = relaxed(rho, v, q)
            ws = WT[q] * scaled
            for p, value in ((q, even + odd), (26 - q, even - odd)):
                post[p, x] = (1.0 - OMEGA) * f[p] + ws * value
        post[13, x] = (1.0 - OMEGA) * f[13] + WT[13] * scaled * still


def row_index(rows, lanes):
    return lax.broadcasted_iota(jnp.int32, (rows, lanes), 0)


def gather(k, x, g, hx, hy, pairs):
    species, planes, rows, lanes = g.shape[1:]
    out = {}
    if 0 in pairs:
        out[0] = g[0, k, x]
    if 1 in pairs:
        out[1] = g[1, k, x - 1] if x > 0 else hx.up(k)
        out[2] = g[2, k, x + 1] if x < planes - 1 else hx.down(k)
    if 3 in pairs:
        flat = g.reshape(7 * species * planes * rows, lanes)
        at = row_index(8, lanes)
        spot = pl.ds(x * species + k, 1)
        for i, step, halo in ((3, -1, hy.up), (4, 1, hy.down)):
            base = ((i * species + k) * planes + x) * rows + step
            parts = [flat[pl.ds(base + t, 8), :] for t in range(0, rows, 8)]
            edge, row = (0, 0) if step < 0 else (-1, 7)
            parts[edge] = jnp.where(at == row, halo(spot, slice(None)), parts[edge])
            out[i] = jnp.concatenate(parts, axis=0)
    if 5 in pairs:
        out[5] = pltpu.roll(g[5, k, x], 1, 1)
        out[6] = pltpu.roll(g[6, k, x], lanes - 1, 1)
    return out


def masks(nt, x):
    rows = nt.shape[1]
    return nt[x] == 1, nt[x, :8, :] == 2, nt[x, rows - 8 :, :] == 3


def settle(value, kind, k, fixed, base):
    _, low, high = kind
    spot = pl.ds(k, 1)
    first = jnp.where(low, fixed[base[0], spot, :], value[:8])
    if value.shape[0] == 8:
        return jnp.where(high, fixed[base[1], spot, :], first)
    last = jnp.where(high, fixed[base[1], spot, :], value[-8:])
    return jnp.concatenate([first, value[8:-8], last] if value.shape[0] > 16 else [first, last], 0)


def walled(moved, kind, k, fixed):
    swap = (0, 2, 1, 4, 3, 6, 5)
    out = {}
    for i, m in moved.items():
        n = {0: 0, 3: 2, 4: 3}.get(i, 1)
        value = m if i == 0 else jnp.where(kind[0], moved[swap[i]], m)
        out[i] = settle(value, kind, k, fixed, (3 + n, 7 + n))
    return out


def inlet_weight(i, side):
    tilt = 4.0 * SPEED * (1.0 if side == 0 else -1.0)
    return {0: 0.25, 3: 0.125 * (1.0 + tilt), 4: 0.125 * (1.0 - tilt)}.get(i, 0.125)


def edge_body(g, hxa, hxb, hya, hyb, nt, u, rx, kc, rk, w, fixed, new, ma, mb, ya, yb, c03, s03,
              rt, odd, keep):
    hx, hy = Halo(hxa, hxb, "gx"), Halo(hya, hyb, "gy")
    species, planes, rows, lanes = g.shape[1:]
    height = c03.shape[1]
    ends = (0, planes - 1)
    flat = g.reshape(7 * species * planes * rows, lanes)
    cflat = c03.reshape(species * height, lanes)
    jump = planes * rows
    zeros = height - 2 * rows
    for k in range(species):
        c03[k, 2 * rows :, :] = jnp.zeros((zeros, lanes), F32)
    for x in range(1, planes - 1):
        for side, row in ((0, 0), (1, rows - 1)):
            kind = nt[x, row : row + 1, :]
            for k, size in bands(species):

                def load(i, plane, r, k=k, size=size):
                    return flat[pl.ds(((i * species + k) * planes + plane) * rows + r, size, jump), :]

                halo = slice(x * species + k, x * species + k + size)
                moved = {
                    0: load(0, x, row),
                    1: load(1, x - 1, row),
                    2: load(2, x + 1, row),
                    3: hy.up(halo, slice(None)) if side == 0 else load(3, x, row - 1),
                    4: hy.down(halo, slice(None)) if side == 1 else load(4, x, row + 1),
                    5: pltpu.roll(load(5, x, row), 1, 1),
                    6: pltpu.roll(load(6, x, row), lanes - 1, 1),
                }
                wide = jnp.broadcast_to(kind, (size, lanes))
                inlet = wide == 2 + side
                value = fixed[1 + side, k : k + size, :]
                total = moved[0]
                for i in range(1, 7):
                    total = total + moved[i]
                total = jnp.where(inlet, value, total)
                i = 3 if side else 4
                kept = jnp.where(wide == 1, moved[7 - i], moved[i])
                kept = jnp.where(inlet, inlet_weight(i, side) * value, kept)
                spot = 2 * rows + 2 * (x - 1) + side
                cflat[pl.ds(k * height + spot, size, height), :] = total
                keep[side, halo, :] = kept
    for n, x in enumerate(ends):
        kind = masks(nt, x)

        def step(k, carry, n=n, x=x, kind=kind):
            moved = gather(k, x, g, hx, hy, (0, 1, 3, 5))
            values = walled(moved, kind, k, fixed)
            total = moved[0]
            for i in range(1, 7):
                total = total + moved[i]
            for i in range(7):
                new[i, k, x] = values[i]
            c03[k, n * rows : (n + 1) * rows, :] = settle(total, kind, k, fixed, (1, 2))
            return carry

        lax.fori_loop(0, species, step, 0, unroll=CONC)
    react(rx, kc, c03, s03, w, rt, odd)
    send_faces(new, rk, c03, s03, [u[0, x] for x in ends], ma, mb)
    send_rows(new, keep, c03, s03, fixed, u, ya, yb)


def rest_body(moving, *refs):
    refs = list(refs)
    g = refs.pop(0) if moving else None
    start, c03, s03, u, rx, kc, rk, w = [refs.pop(0) for _ in range(8)]
    if moving:
        hya, hyb, nt, fixed = [refs.pop(0) for _ in range(4)]
        hy = Halo(hya, hyb, "gy")
    new, c12, s12, rt = refs
    species, planes, rows, _ = new.shape[1:]
    for x in range(1, planes - 1):
        kind = masks(nt, x) if moving else None

        def step(k, carry, x=x, kind=kind):
            if moving:
                moved = gather(k, x, g, None, hy, (0, 1, 3, 5))
                values = walled(moved, kind, k, fixed)
            else:
                moved = {i: start[i, k, x] for i in range(7)}
            total = moved[0]
            for i in range(1, 7):
                total = total + moved[i]
            if moving:
                for i in range(7):
                    new[i, k, x] = values[i]
                total = settle(total, kind, k, fixed, (1, 2))
            c12[k, (x - 1) * rows : x * rows, :] = total
            return carry

        lax.fori_loop(0, species, step, 0, unroll=CONC)
    react(rx, kc, c12, s12, w, rt)
    for x in range(planes):
        ux, uy, uz = 0.5 * u[0, x], 0.5 * u[1, x], 0.5 * u[2, x]
        if x in (0, planes - 1):
            cr, sr, half = c03, s03, slice((x > 0) * rows, (x > 0) * rows + rows)
        else:
            cr, sr, half = c12, s12, slice((x - 1) * rows, x * rows)

        def collide(k, carry, x=x, cr=cr, sr=sr, half=half, ux=ux, uy=uy, uz=uz):
            r = rk[k]
            keep = 1.0 - r
            a = r * cr[k, half, :]
            base1 = 0.125 * (a + sr[k, half, :])
            new[0, k, x] = keep * new[0, k, x] + (base1 + base1)
            for i, v in ((1, ux), (3, uy), (5, uz)):
                d = a * v
                up = keep * new[i, k, x] + (base1 + d)
                down = keep * new[i + 1, k, x] + (base1 - d)
                new[i, k, x] = up
                new[i + 1, k, x] = down
            return carry

        lax.fori_loop(0, species, collide, 0, unroll=5)


def faces_body(species, post, hya, hyb, fa, fb):
    planes = post.shape[1]
    hy = Halo(hya, hyb, "gy")
    even = is_even("gx")
    for n in range(9):
        high = flow_moved(UPX[n], planes - 1, post, hy, species * planes)
        low = flow_moved(DNX[n], 0, post, hy, species * planes)
        fa[n] = pick(even, high, low)
        fb[n] = pick(even, low, high)


def flow_moved(q, src, post, hy, base):
    planes, rows, lanes = post.shape[1:]
    at = row_index(rows, lanes)
    step = VEL[q][1]
    value = post[q, src]
    if step:
        row, queue, halo = (0, UPY, hy.up) if step > 0 else (rows - 1, DNY, hy.down)
        spot = base + queue.index(q) * planes + src
        shifted = pltpu.roll(value, step % rows, 0)
        value = jnp.where(at == row, halo(slice(spot, spot + 1), slice(None)), shifted)
    return value


def flow_end_body(species, post, fxa, fxb, hya, hyb, nt, result, out, sem):
    planes, _, lanes = post.shape[1:]
    base = species * planes
    hx, hy = Halo(fxa, fxb, "gx"), Halo(hya, hyb, "gy")
    copies = []
    for x in list(range(1, planes - 1)) + [0, planes - 1]:
        kind = nt[x]
        wall = kind == 1
        inlet = kind >= 2
        fuel = kind == 2
        for q in range(13, 27):
            moved = {}
            for p in {q, 26 - q}:
                a, _, c = VEL[p]
                src = x - a
                if src < 0:
                    value = hx.up(UPX.index(p))
                elif src >= planes:
                    value = hx.down(DNX.index(p))
                else:
                    value = flow_moved(p, src, post, hy, base)
                if c:
                    value = pltpu.roll(value, 1 if c > 0 else lanes - 1, 1)
                moved[p] = value
            for p in moved:
                cu = VEL[p][1] * SPEED
                fixed = [
                    WT[p] * (1.0 + 3.0 * s * cu + 4.5 * cu * cu - 1.5 * SPEED * SPEED)
                    for s in (1.0, -1.0)
                ]
                value = moved[p] if p == 13 else jnp.where(wall, moved[26 - p], moved[p])
                out[p, x] = jnp.where(inlet, jnp.where(fuel, fixed[0], fixed[1]), value)
        copies.append(pltpu.make_async_copy(out.at[:, x], result.at[:, x], sem.at[x]))
        copies[-1].start()
    for copy in copies:
        copy.wait()


def end_body(mode, *refs):
    refs = list(refs)
    g = refs.pop(0)
    hx = Halo(refs.pop(0), refs.pop(0), "gx") if mode == 1 else None
    hy = Halo(refs.pop(0), refs.pop(0), "gy") if mode == 3 else None
    nt, fixed = [refs.pop(0) for _ in range(2)]
    if mode:
        refs.pop(0)
    out, buf, sem = refs
    species, planes = g.shape[1:3]
    inner = range(1, planes - 1)
    cover = {
        0: {0: range(planes), 5: range(planes), 1: inner},
        3: {3: range(planes)},
        1: {1: (0, planes - 1)},
    }[mode]
    chunk = 5 if species % 5 == 0 else 1
    copies = []
    for start in range(0, species, chunk):
        for x in range(planes):
            pairs = [p for p, xs in cover.items() if x in xs]
            if not pairs:
                continue
            kind = masks(nt, x)

            def step(k, carry, x=x, pairs=pairs, kind=kind):
                values = walled(gather(k, x, g, hx, hy, pairs), kind, k, fixed)
                for i, value in values.items():
                    buf[i - mode, k, x] = value
                return carry

            lax.fori_loop(start, start + chunk, step, 0, unroll=True)
        part = slice(start, start + chunk)
        for pair in cover:
            for i in (0,) if pair == 0 else (pair, pair + 1):
                if pair != 1:
                    spans = [slice(0, planes)]
                elif mode == 0:
                    spans = [slice(1, planes - 1)]
                else:
                    spans = [slice(0, 1), slice(planes - 1, planes)]
                for span in spans:
                    copies.append(
                        pltpu.make_async_copy(
                            buf.at[i - mode, part, span], out.at[i, part, span], sem.at[len(copies)]
                        )
                    )
                    copies[-1].start()
    for copy in copies:
        copy.wait()


def per_device(populations, species, node_type, reactions, rate_const, species_rate, inlet_mix):
    planes, rows, lanes = node_type.shape
    count = species.shape[1]
    total = reactions.shape[0]
    pad = total % 2
    if pad:
        reactions = jnp.pad(reactions, ((0, pad), (0, 0)))
        rate_const = jnp.pad(rate_const, (0, pad))
        total += pad
    nt = inv(node_type)
    smem = [SM] * 3

    def arr(*shape):
        return VMEM(shape, F32)

    state = arr(7, count, planes, rows, lanes)
    inner = planes - 2
    edges = -(-2 * inner // 8) * 8
    wide = (2 * rows + edges) // 8
    react_out = arr(count, 2 * rows + edges, lanes)
    rates = VMEM((2 * total * 8, wide // 2 * 2 * lanes), BF16)
    odd = VMEM((total * 8, 2 * lanes), BF16)
    rates_in = VMEM((2 * total * 8, inner * rows // 8 * lanes), BF16)
    inside = VMEM((count, inner * rows, lanes), F32)

    def swap(near, far, axis):
        size = lax.axis_size(axis)
        far = lax.ppermute(far, axis, pairs(size, False))
        near = lax.ppermute(near, axis, pairs(size, True))
        return near, far

    xmsg = arr(count, rows, lanes)
    sems = [pltpu.SemaphoreType.DMA((planes,)), pltpu.SemaphoreType.DMA((planes,))]
    ints = pltpu.SMEM((3, total), jnp.int32)
    flows = arr(27, planes, rows, lanes)
    ymsg = arr((count + 9) * planes, lanes)
    keep = VMEM((2, count * planes, lanes), F32)
    sv, w, ma, mb, ya, yb, c03, s03, fixed, u, post, *tables = call(
        first_body,
        [hbm(v) for v in (populations, species, reactions.T, rate_const, species_rate, inlet_mix)],
        [ANY] * 6,
        (flows, state, VMEM((count * 8, 2 * total * 8), BF16), xmsg, xmsg, ymsg, ymsg, react_out,
         react_out, arr(11, count, lanes), arr(3, planes, rows, lanes), flows, ints,
         pltpu.SMEM((total,), F32), pltpu.SMEM((count,), F32))[1:],
        [VM] * 11 + [SM] * 3,
        [pltpu.SMEM((2, count), F32), rates, odd, keep, VMEM((3, total), jnp.int32)] + sems
        + [pltpu.SemaphoreType.DMA((5,)), flows],
    )
    tables = [pltpu.with_memory_space_constraint(v, pltpu.SMEM) for v in tables]
    hx = swap(ma, mb, "gx")
    hy = swap(ya, yb, "gy")
    ymsg = arr(count * planes, lanes)
    flow_hy = hy
    g = None
    new = sv
    for s in range(SUBSTEPS):
        moving = s > 0
        if moving:
            halo = hy
            new, ma, mb, ya, yb, c03, s03 = call(
                edge_body,
                [inv(v) for v in (g, *hx, *hy, node_type, u)] + tables + [inv(w), inv(fixed)],
                [VM] * 7 + smem + [VM] * 2,
                (state, xmsg, xmsg, ymsg, ymsg, react_out, react_out),
                [VM] * 7,
                [rates, odd, keep],
            )
            hx = swap(ma, mb, "gx")
            hy = swap(ya, yb, "gy")
        ins = ([inv(g)] if moving else []) + [inv(v) for v in (new, c03, s03, u)]
        ins += tables + [inv(w)]
        specs = [VM] * (5 if moving else 4) + smem + [VM]
        if moving:
            ins += [inv(v) for v in (*halo, node_type, fixed)]
        specs += [VM] * (len(ins) - len(specs))
        (g,) = call(
            functools.partial(rest_body, moving),
            ins,
            specs,
            (state,),
            [VM],
            [inside, inside, rates_in],
            alias={1 if moving else 0: 0},
        )
        if not moving:
            face = arr(9, rows, lanes)
            sent = call(
                functools.partial(faces_body, count),
                [inv(v) for v in (post, *hy)],
                [VM] * 3,
                (face, face),
                [VM] * 2,
            )
            flow_hx = swap(*sent, "gx")
    new_populations = call(
        functools.partial(flow_end_body, count),
        [inv(v) for v in (post, *flow_hx, *flow_hy, node_type)],
        [VM] * 6,
        pltpu.HBM((27, planes, rows, lanes), F32),
        ANY,
        [flows, sems[0]],
    )
    result = None
    for mode, extra in ((0, ()), (3, hy), (1, hx)):
        ins = [inv(v) for v in (g,) + extra] + [nt, inv(fixed)] + ([hbm(result)] if mode else [])
        result = call(
            functools.partial(end_body, mode),
            ins,
            [VM] * (3 + len(extra)) + ([ANY] if mode else []),
            pltpu.HBM((7, count, planes, rows, lanes), F32),
            ANY,
            [VMEM((7 if mode == 0 else 2, count, planes, rows, lanes), F32),
             pltpu.SemaphoreType.DMA((32,))],
            alias={len(ins) - 1: 0} if mode else None,
        )
    return new_populations, result


def solution(mesh):
    flow = P(None, "gx", "gy", None)
    kinds = P(None, None, "gx", "gy", None)
    return jax.shard_map(
        per_device,
        mesh=mesh,
        in_specs=(flow, kinds, P("gx", "gy", None), P(), P(), P(), P()),
        out_specs=(flow, kinds),
        check_vma=False,
    )
```

```python
import functools

import jax
import jax.numpy as jnp
from jax import lax
from jax.experimental import pallas as pl
from jax.experimental.pallas import tpu as pltpu
from jax.sharding import PartitionSpec as P


SUBSTEPS = 3
CONC = 20
OMEGA = 1.6
SPEED = 0.05
F32 = jnp.float32
BF16 = jnp.bfloat16
VEL = [(a, b, c) for a in (-1, 0, 1) for b in (-1, 0, 1) for c in (-1, 0, 1)]
WT = [(8.0 / 27, 2.0 / 27, 1.0 / 54, 1.0 / 216)[abs(a) + abs(b) + abs(c)] for a, b, c in VEL]
UPX = [q for q in range(27) if VEL[q][0] > 0]
DNX = [q for q in range(27) if VEL[q][0] < 0]
UPY = [q for q in range(27) if VEL[q][1] > 0]
DNY = [q for q in range(27) if VEL[q][1] < 0]
MIB = 1 << 20
VMEM = pltpu.VMEM
VM = pl.BlockSpec(memory_space=pltpu.VMEM)
SM = pl.BlockSpec(memory_space=pltpu.SMEM)
ANY = pl.BlockSpec(memory_space=pl.ANY)


def inv(x):
    return pltpu.with_memory_space_constraint(x, pltpu.VMEM)


def hbm(x):
    return pltpu.with_memory_space_constraint(x, pltpu.HBM)


def pairs(size, near):
    if near:
        return [(i, i ^ 1) for i in range(size)]
    return [(i, (i + 1 if i % 2 else i - 1) % size) for i in range(size)]


def is_even(axis):
    return lax.rem(lax.axis_index(axis), 2) == 0


def pick(even, one, other):
    return jnp.where(even, one, other)


class Halo:
    def __init__(self, near, far, axis):
        self.near, self.far, self.even = near, far, is_even(axis)

    def up(self, *at):
        return pick(self.even, self.far[at], self.near[at])

    def down(self, *at):
        return pick(self.even, self.near[at], self.far[at])


def call(body, ins, specs, outs, out_specs, scratch=(), alias=None, mib=12, cost=2_000_000):
    return pl.pallas_call(
        body,
        out_shape=outs,
        in_specs=specs,
        out_specs=out_specs,
        scratch_shapes=list(scratch),
        input_output_aliases=alias or {},
        compiler_params=pltpu.CompilerParams(vmem_limit_bytes=mib * MIB),
        cost_estimate=pl.CostEstimate(flops=cost, bytes_accessed=cost, transcendentals=0),
    )(*ins)


def react(rx, kc, c_ref, s_ref, w_ref, rt_ref, odd_ref=None, start=0, stop=None):
    species, rows, lanes = c_ref.shape
    part = slice(start, stop or rows)
    tiles = (part.stop - part.start) // 8
    half = w_ref.shape[1] // 2
    even = tiles - tiles % 2
    for j in range(half // 8):
        rate = c_ref[rx[0, j], part, :] * (c_ref[rx[1, j], part, :] * kc[j])
        at = slice(8 * j, 8 * j + 8)
        for t in range(0, even, 2):
            both = jnp.concatenate([rate[8 * t : 8 * t + 8], rate[8 * t + 8 : 8 * t + 16]], axis=1)
            high = both.astype(BF16)
            low = (both - high.astype(F32)).astype(BF16)
            rt_ref[at, lanes * t : lanes * (t + 2)] = high
            rt_ref[half + 8 * j : half + 8 * j + 8, lanes * t : lanes * (t + 2)] = low
        if even < tiles:
            last = rate[8 * even :]
            rest = last - last.astype(BF16).astype(F32)
            odd_ref[at, :] = jnp.concatenate([last, rest], axis=1).astype(BF16)
    if even < tiles:
        total = jnp.dot(w_ref[:, :half], odd_ref[...], preferred_element_type=F32)
        total = total[:, :lanes] + total[:, lanes:]
        s_ref[:, start + 8 * even : start + 8 * tiles, :] = total.reshape(species, 8, lanes)
    if even:
        total = jnp.dot(w_ref[...], rt_ref[:, : lanes * even], preferred_element_type=F32)
        for t in range(even):
            s_ref[:, start + 8 * t : start + 8 * t + 8, :] = total[
                :, lanes * t : lanes * (t + 1)
            ].reshape(species, 8, lanes)


def moments(f):
    rho = f[0]
    for q in range(1, 27):
        rho = rho + f[q]
    parts = []
    for axis in range(3):
        plus = None
        for q in range(27):
            if VEL[q][axis] > 0:
                diff = f[q] - f[26 - q]
                plus = diff if plus is None else plus + diff
        parts.append(plus)
    scale = 1.0 / rho
    return rho, [p * scale for p in parts]


def cross(g, rk, c, s, ux, sign):
    a = rk * c
    return (1.0 - rk) * g + (0.125 * (a + s) + (0.5 * sign) * (a * ux))


def bands(species):
    return [(k, min(8, species - k)) for k in range(0, species, 8)]


def stoichiometry(rv, w):
    rows, width = w.shape
    half = width // 2
    species, total = rows // 8, half // 8

    def iota(shape, axis):
        return lax.broadcasted_iota(jnp.int32, shape, axis)

    def hot(test):
        return jnp.where(test, 1.0, 0.0)

    label = iota((species, total), 0)
    net = hot(rv[2:3, :] == label) - hot(rv[0:1, :] == label) - hot(rv[1:2, :] == label)
    tall = hot((iota((rows, species), 0) >> 3) == iota((rows, species), 1)).astype(BF16)
    wide = hot((iota((total, half), 1) >> 3) == iota((total, half), 0)).astype(BF16)
    part = jnp.dot(tall, net.astype(BF16), preferred_element_type=F32)
    full = jnp.dot(part.astype(BF16), wide, preferred_element_type=F32)
    same = (iota((rows, half), 0) & 7) == (iota((rows, half), 1) & 7)
    full = jnp.where(same, full, 0.0).astype(BF16)
    w[:, :half] = full
    w[:, half:] = full


def first_body(pop, spec, react_in, kc_in, rk_in, mix_in, sv, w, ma, mb, ya, yb, c03, s03,
               fixed, u, post, rx, kc, rk, mix, rt, odd, keep, rv, psem, ssem, tsem, pv):
    planes, rows, lanes = pop.shape[1:]
    species = spec.shape[1]
    ends = (0, planes - 1)
    inner = range(1, planes - 1)
    small = [
        pltpu.make_async_copy(src, dst, tsem.at[n])
        for n, (src, dst) in enumerate(
            ((react_in, rv), (react_in, rx), (kc_in, kc), (rk_in, rk), (mix_in, mix))
        )
    ]
    kinds = [pltpu.make_async_copy(spec.at[:, :, x], sv.at[:, :, x], ssem.at[x])
             for x in range(planes)]
    flows = [pltpu.make_async_copy(pop.at[:, x], pv.at[:, x], psem.at[x]) for x in range(planes)]
    for copy in small + [kinds[x] for x in ends] + flows + [kinds[x] for x in inner]:
        copy.start()
    for k in range(species):
        c03[k, 2 * rows :, :] = jnp.zeros((c03.shape[1] - 2 * rows, lanes), F32)
    for copy in small:
        copy.wait()
    stoichiometry(rv, w)
    for k in range(species):
        for n, value in enumerate((rk[k], mix[0, k], mix[1, k])):
            fixed[n, k : k + 1, :] = jnp.full((1, lanes), value, F32)
    for side in range(2):
        for n, i in enumerate((0, 1, 3, 4)):
            fixed[3 + 4 * side + n] = inlet_weight(i, side) * fixed[1 + side]
    for n, x in enumerate(ends):
        kinds[x].wait()

        def conc(k, carry, n=n, x=x):
            total = sv[0, k, x]
            for i in range(1, 7):
                total = total + sv[i, k, x]
            c03[k, n * rows : (n + 1) * rows, :] = total
            return carry

        lax.fori_loop(0, species, conc, 0, unroll=5)
    react(rx, kc, c03, s03, w, rt, start=0, stop=2 * rows)
    for copy in flows:
        copy.wait()
    collide_flow(pv, u, post)
    for x in inner:
        kinds[x].wait()
    flat = sv.reshape(7 * species * planes * rows, lanes)
    height = c03.shape[1]
    cflat = c03.reshape(species * height, lanes)
    for x in inner:
        for side, row in ((0, 0), (1, rows - 1)):
            for k, size in bands(species):
                values = [
                    flat[pl.ds(((i * species + k) * planes + x) * rows + row, size, planes * rows), :]
                    for i in range(7)
                ]
                total = values[0]
                for i in range(1, 7):
                    total = total + values[i]
                spot = 2 * rows + 2 * (x - 1) + side
                cflat[pl.ds(k * height + spot, size, height), :] = total
                keep[side, x * species + k : x * species + k + size, :] = values[3 if side else 4]
    react(rx, kc, c03, s03, w, rt, odd, start=2 * rows)
    send_faces(sv, rk, c03, s03, [u[0, x] for x in ends], ma, mb)
    send_rows(sv, keep, c03, s03, fixed, u, ya, yb)
    first, last, even = edge_flags()
    for n in range(9):
        for x in range(planes):
            at = slice((species + n) * planes + x, (species + n) * planes + x + 1)
            top = jnp.where(last, 0.0, post[UPY[n], x, rows - 1 : rows, :])
            bottom = jnp.where(first, 0.0, post[DNY[n], x, 0:1, :])
            ya[at, :] = pick(even, top, bottom)
            yb[at, :] = pick(even, bottom, top)


def edge_flags():
    rank, size = lax.axis_index("gy"), lax.axis_size("gy")
    return rank == 0, rank == size - 1, is_even("gy")


def send_rows(state, keep, c03, s03, fixed, u, ya, yb):
    species, planes, rows, lanes = state.shape[1:]
    height = c03.shape[1]
    fresh = state.reshape(7 * species * planes * rows, lanes)
    cflat = c03.reshape(species * height, lanes)
    sflat = s03.reshape(species * height, lanes)
    first, last, even = edge_flags()
    for x in range(planes):
        for k, size in bands(species):
            halo = slice(x * species + k, x * species + k + size)
            sent = []
            for side, row, off in ((0, 0, first), (1, rows - 1, last)):
                i, sign = (3, 1.0) if side else (4, -1.0)
                if x in (0, planes - 1):
                    spot = (x > 0) * rows + row
                    at = ((i * species + k) * planes + x) * rows + row
                    value = fresh[pl.ds(at, size, planes * rows), :]
                else:
                    spot = 2 * rows + 2 * (x - 1) + side
                    value = keep[side, halo, :]
                c = cflat[pl.ds(k * height + spot, size, height), :]
                s = sflat[pl.ds(k * height + spot, size, height), :]
                uy = u[1, x, row : row + 1, :]
                value = cross(value, fixed[0, k : k + size, :], c, s, uy, sign)
                sent.append(jnp.where(off, 0.0, value))
            ya[halo, :] = pick(even, sent[1], sent[0])
            yb[halo, :] = pick(even, sent[0], sent[1])


def send_faces(state, rk, c03, s03, speeds, ma, mb):
    species, planes, rows = state.shape[1:4]
    even = is_even("gx")

    def send(k, carry):
        low = cross(state[2, k, 0], rk[k], c03[k, :rows, :], s03[k, :rows, :], speeds[0], -1.0)
        part = slice(rows, 2 * rows)
        high = cross(
            state[1, k, planes - 1], rk[k], c03[k, part, :], s03[k, part, :], speeds[1], 1.0
        )
        ma[k] = pick(even, high, low)
        mb[k] = pick(even, low, high)
        return carry

    lax.fori_loop(0, species, send, 0, unroll=5)


def relaxed(rho, v, q):
    still = 1.0 - 1.5 * (v[0] * v[0] + v[1] * v[1] + v[2] * v[2])
    along = None
    for axis in range(3):
        if VEL[q][axis]:
            term = v[axis] if VEL[q][axis] > 0 else -v[axis]
            along = term if along is None else along + term
    return still, OMEGA * rho, (still + 4.5 * along * along, 3.0 * along)


def collide_flow(pv, u, post):
    for x in range(pv.shape[1]):
        f = [pv[q, x] for q in range(27)]
        rho, v = moments(f)
        for axis in range(3):
            u[axis, x] = v[axis]
        for q in range(14, 27):
            still, scaled, (even, odd) = relaxed(rho, v, q)
            ws = WT[q] * scaled
            for p, value in ((q, even + odd), (26 - q, even - odd)):
                post[p, x] = (1.0 - OMEGA) * f[p] + ws * value
        post[13, x] = (1.0 - OMEGA) * f[13] + WT[13] * scaled * still


def row_index(rows, lanes):
    return lax.broadcasted_iota(jnp.int32, (rows, lanes), 0)


def gather(k, x, g, hx, hy, pairs):
    species, planes, rows, lanes = g.shape[1:]
    out = {}
    if 0 in pairs:
        out[0] = g[0, k, x]
    if 1 in pairs:
        out[1] = g[1, k, x - 1] if x > 0 else hx.up(k)
        out[2] = g[2, k, x + 1] if x < planes - 1 else hx.down(k)
    if 3 in pairs:
        flat = g.reshape(7 * species * planes * rows, lanes)
        at = row_index(8, lanes)
        spot = pl.ds(x * species + k, 1)
        for i, step, halo in ((3, -1, hy.up), (4, 1, hy.down)):
            base = ((i * species + k) * planes + x) * rows + step
            parts = [flat[pl.ds(base + t, 8), :] for t in range(0, rows, 8)]
            edge, row = (0, 0) if step < 0 else (-1, 7)
            parts[edge] = jnp.where(at == row, halo(spot, slice(None)), parts[edge])
            out[i] = jnp.concatenate(parts, axis=0)
    if 5 in pairs:
        out[5] = pltpu.roll(g[5, k, x], 1, 1)
        out[6] = pltpu.roll(g[6, k, x], lanes - 1, 1)
    return out


def masks(nt, x):
    rows = nt.shape[1]
    return nt[x] == 1, nt[x, :8, :] == 2, nt[x, rows - 8 :, :] == 3


def settle(value, kind, k, fixed, base):
    _, low, high = kind
    spot = pl.ds(k, 1)
    first = jnp.where(low, fixed[base[0], spot, :], value[:8])
    if value.shape[0] == 8:
        return jnp.where(high, fixed[base[1], spot, :], first)
    last = jnp.where(high, fixed[base[1], spot, :], value[-8:])
    return jnp.concatenate([first, value[8:-8], last] if value.shape[0] > 16 else [first, last], 0)


def walled(moved, kind, k, fixed):
    swap = (0, 2, 1, 4, 3, 6, 5)
    out = {}
    for i, m in moved.items():
        n = {0: 0, 3: 2, 4: 3}.get(i, 1)
        value = m if i == 0 else jnp.where(kind[0], moved[swap[i]], m)
        out[i] = settle(value, kind, k, fixed, (3 + n, 7 + n))
    return out


def inlet_weight(i, side):
    tilt = 4.0 * SPEED * (1.0 if side == 0 else -1.0)
    return {0: 0.25, 3: 0.125 * (1.0 + tilt), 4: 0.125 * (1.0 - tilt)}.get(i, 0.125)


def edge_body(g, hxa, hxb, hya, hyb, nt, u, rx, kc, rk, w, fixed, new, ma, mb, ya, yb, c03, s03,
              rt, odd, keep):
    hx, hy = Halo(hxa, hxb, "gx"), Halo(hya, hyb, "gy")
    species, planes, rows, lanes = g.shape[1:]
    height = c03.shape[1]
    ends = (0, planes - 1)
    flat = g.reshape(7 * species * planes * rows, lanes)
    cflat = c03.reshape(species * height, lanes)
    jump = planes * rows
    zeros = height - 2 * rows
    for k in range(species):
        c03[k, 2 * rows :, :] = jnp.zeros((zeros, lanes), F32)
    for x in range(1, planes - 1):
        for side, row in ((0, 0), (1, rows - 1)):
            kind = nt[x, row : row + 1, :]
            for k, size in bands(species):

                def load(i, plane, r, k=k, size=size):
                    return flat[pl.ds(((i * species + k) * planes + plane) * rows + r, size, jump), :]

                halo = slice(x * species + k, x * species + k + size)
                moved = {
                    0: load(0, x, row),
                    1: load(1, x - 1, row),
                    2: load(2, x + 1, row),
                    3: hy.up(halo, slice(None)) if side == 0 else load(3, x, row - 1),
                    4: hy.down(halo, slice(None)) if side == 1 else load(4, x, row + 1),
                    5: pltpu.roll(load(5, x, row), 1, 1),
                    6: pltpu.roll(load(6, x, row), lanes - 1, 1),
                }
                wide = jnp.broadcast_to(kind, (size, lanes))
                inlet = wide == 2 + side
                value = fixed[1 + side, k : k + size, :]
                total = moved[0]
                for i in range(1, 7):
                    total = total + moved[i]
                total = jnp.where(inlet, value, total)
                i = 3 if side else 4
                kept = jnp.where(wide == 1, moved[7 - i], moved[i])
                kept = jnp.where(inlet, inlet_weight(i, side) * value, kept)
                spot = 2 * rows + 2 * (x - 1) + side
                cflat[pl.ds(k * height + spot, size, height), :] = total
                keep[side, halo, :] = kept
    for n, x in enumerate(ends):
        kind = masks(nt, x)

        def step(k, carry, n=n, x=x, kind=kind):
            moved = gather(k, x, g, hx, hy, (0, 1, 3, 5))
            values = walled(moved, kind, k, fixed)
            total = moved[0]
            for i in range(1, 7):
                total = total + moved[i]
            for i in range(7):
                new[i, k, x] = values[i]
            c03[k, n * rows : (n + 1) * rows, :] = settle(total, kind, k, fixed, (1, 2))
            return carry

        lax.fori_loop(0, species, step, 0, unroll=CONC)
    react(rx, kc, c03, s03, w, rt, odd)
    send_faces(new, rk, c03, s03, [u[0, x] for x in ends], ma, mb)
    send_rows(new, keep, c03, s03, fixed, u, ya, yb)


def rest_body(moving, final, *refs):
    refs = list(refs)
    g = refs.pop(0) if moving else None
    start, c03, s03, u, rx, kc, rk, w = [refs.pop(0) for _ in range(8)]
    if moving:
        hya, hyb, nt, fixed = [refs.pop(0) for _ in range(4)]
        hy = Halo(hya, hyb, "gy")
    new = refs.pop(0)
    result = refs.pop(0) if final else None
    c12, s12, rt = refs[:3]
    species, planes, rows, _ = new.shape[1:]
    for x in range(1, planes - 1):
        kind = masks(nt, x) if moving else None

        def step(k, carry, x=x, kind=kind):
            if moving:
                moved = gather(k, x, g, None, hy, (0, 1, 3, 5))
                values = walled(moved, kind, k, fixed)
            else:
                moved = {i: start[i, k, x] for i in range(7)}
            total = moved[0]
            for i in range(1, 7):
                total = total + moved[i]
            if moving:
                for i in range(7):
                    new[i, k, x] = values[i]
                total = settle(total, kind, k, fixed, (1, 2))
            c12[k, (x - 1) * rows : x * rows, :] = total
            return carry

        lax.fori_loop(0, species, step, 0, unroll=CONC)
    react(rx, kc, c12, s12, w, rt)
    chunk = 5 if final and species % 5 == 0 else species
    copies = []
    for begin in range(0, species, chunk):
        end = begin + chunk
        for x in range(planes):
            ux, uy, uz = 0.5 * u[0, x], 0.5 * u[1, x], 0.5 * u[2, x]
            if x in (0, planes - 1):
                cr, sr, half = c03, s03, slice((x > 0) * rows, (x > 0) * rows + rows)
            else:
                cr, sr, half = c12, s12, slice((x - 1) * rows, x * rows)

            def collide(k, carry, x=x, cr=cr, sr=sr, half=half, ux=ux, uy=uy, uz=uz):
                r = rk[k]
                keep = 1.0 - r
                a = r * cr[k, half, :]
                base1 = 0.125 * (a + sr[k, half, :])
                new[0, k, x] = keep * new[0, k, x] + (base1 + base1)
                for i, v in ((1, ux), (3, uy), (5, uz)):
                    d = a * v
                    up = keep * new[i, k, x] + (base1 + d)
                    down = keep * new[i + 1, k, x] + (base1 - d)
                    new[i, k, x] = up
                    new[i + 1, k, x] = down
                return carry

            lax.fori_loop(begin, end, collide, 0, unroll=5)
        if final:
            copies += put_out(
                {0: range(planes), 5: range(planes), 1: range(1, planes - 1)},
                slice(begin, end), new, None, None, nt, fixed, result, refs[3], refs[4], len(copies),
            )
    for copy in copies:
        copy.wait()


def put_out(cover, part, g, hx, hy, nt, fixed, result, buf, sem, used):
    planes = g.shape[2]
    for x in range(planes):
        pairs = [p for p, xs in cover.items() if x in xs]
        kind = masks(nt, x)
        for k in range(part.start, part.stop):
            values = walled(gather(k, x, g, hx, hy, pairs), kind, k, fixed)
            for i, value in values.items():
                buf[i, k, x] = value
    copies = []
    for pair, xs in cover.items():
        for i in (0,) if pair == 0 else (pair, pair + 1):
            if len(xs) == planes or 0 not in xs:
                spans = [slice(xs[0], xs[-1] + 1)]
            else:
                spans = [slice(x, x + 1) for x in xs]
            for span in spans:
                at = (i, part, span)
                copies.append(
                    pltpu.make_async_copy(buf.at[at], result.at[at], sem.at[used + len(copies)])
                )
    for copy in copies:
        copy.start()
    return copies


def faces_body(species, post, hya, hyb, fa, fb):
    planes = post.shape[1]
    hy = Halo(hya, hyb, "gy")
    even = is_even("gx")
    for n in range(9):
        high = flow_moved(UPX[n], planes - 1, post, hy, species * planes)
        low = flow_moved(DNX[n], 0, post, hy, species * planes)
        fa[n] = pick(even, high, low)
        fb[n] = pick(even, low, high)


def flow_moved(q, src, post, hy, base):
    planes, rows, lanes = post.shape[1:]
    at = row_index(rows, lanes)
    step = VEL[q][1]
    value = post[q, src]
    if step:
        row, queue, halo = (0, UPY, hy.up) if step > 0 else (rows - 1, DNY, hy.down)
        spot = base + queue.index(q) * planes + src
        shifted = pltpu.roll(value, step % rows, 0)
        value = jnp.where(at == row, halo(slice(spot, spot + 1), slice(None)), shifted)
    return value


def flow_end_body(species, post, fxa, fxb, hya, hyb, nt, result, out, sem):
    planes, _, lanes = post.shape[1:]
    base = species * planes
    hx, hy = Halo(fxa, fxb, "gx"), Halo(hya, hyb, "gy")
    copies = []
    for x in list(range(1, planes - 1)) + [0, planes - 1]:
        kind = nt[x]
        wall = kind == 1
        inlet = kind >= 2
        fuel = kind == 2
        for q in range(13, 27):
            moved = {}
            for p in {q, 26 - q}:
                a, _, c = VEL[p]
                src = x - a
                if src < 0:
                    value = hx.up(UPX.index(p))
                elif src >= planes:
                    value = hx.down(DNX.index(p))
                else:
                    value = flow_moved(p, src, post, hy, base)
                if c:
                    value = pltpu.roll(value, 1 if c > 0 else lanes - 1, 1)
                moved[p] = value
            for p in moved:
                cu = VEL[p][1] * SPEED
                fixed = [
                    WT[p] * (1.0 + 3.0 * s * cu + 4.5 * cu * cu - 1.5 * SPEED * SPEED)
                    for s in (1.0, -1.0)
                ]
                value = moved[p] if p == 13 else jnp.where(wall, moved[26 - p], moved[p])
                out[p, x] = jnp.where(inlet, jnp.where(fuel, fixed[0], fixed[1]), value)
        copies.append(pltpu.make_async_copy(out.at[:, x], result.at[:, x], sem.at[x]))
        copies[-1].start()
    for copy in copies:
        copy.wait()


def end_body(g, hxa, hxb, hya, hyb, nt, fixed, before, out, buf, sem):
    del before
    species, planes = g.shape[1:3]
    hx, hy = Halo(hxa, hxb, "gx"), Halo(hya, hyb, "gy")
    chunk = 5 if species % 5 == 0 else species
    copies = []
    for begin in range(0, species, chunk):
        copies += put_out(
            {3: range(planes), 1: (0, planes - 1)},
            slice(begin, begin + chunk), g, hx, hy, nt, fixed, out, buf, sem, len(copies),
        )
    for copy in copies:
        copy.wait()


def per_device(populations, species, node_type, reactions, rate_const, species_rate, inlet_mix):
    planes, rows, lanes = node_type.shape
    count = species.shape[1]
    total = reactions.shape[0]
    pad = total % 2
    if pad:
        reactions = jnp.pad(reactions, ((0, pad), (0, 0)))
        rate_const = jnp.pad(rate_const, (0, pad))
        total += pad
    nt = inv(node_type)
    smem = [SM] * 3

    def arr(*shape):
        return VMEM(shape, F32)

    state = arr(7, count, planes, rows, lanes)
    inner = planes - 2
    edges = -(-2 * inner // 8) * 8
    wide = (2 * rows + edges) // 8
    react_out = arr(count, 2 * rows + edges, lanes)
    rates = VMEM((2 * total * 8, wide // 2 * 2 * lanes), BF16)
    odd = VMEM((total * 8, 2 * lanes), BF16)
    rates_in = VMEM((2 * total * 8, inner * rows // 8 * lanes), BF16)
    inside = VMEM((count, inner * rows, lanes), F32)

    def swap(near, far, axis):
        size = lax.axis_size(axis)
        far = lax.ppermute(far, axis, pairs(size, False))
        near = lax.ppermute(near, axis, pairs(size, True))
        return near, far

    xmsg = arr(count, rows, lanes)
    sems = [pltpu.SemaphoreType.DMA((planes,)), pltpu.SemaphoreType.DMA((planes,))]
    ints = pltpu.SMEM((3, total), jnp.int32)
    flows = arr(27, planes, rows, lanes)
    ymsg = arr((count + 9) * planes, lanes)
    keep = VMEM((2, count * planes, lanes), F32)
    sv, w, ma, mb, ya, yb, c03, s03, fixed, u, post, *tables = call(
        first_body,
        [hbm(v) for v in (populations, species, reactions.T, rate_const, species_rate, inlet_mix)],
        [ANY] * 6,
        (flows, state, VMEM((count * 8, 2 * total * 8), BF16), xmsg, xmsg, ymsg, ymsg, react_out,
         react_out, arr(11, count, lanes), arr(3, planes, rows, lanes), flows, ints,
         pltpu.SMEM((total,), F32), pltpu.SMEM((count,), F32))[1:],
        [VM] * 11 + [SM] * 3,
        [pltpu.SMEM((2, count), F32), rates, odd, keep, VMEM((3, total), jnp.int32)] + sems
        + [pltpu.SemaphoreType.DMA((5,)), flows],
    )
    tables = [pltpu.with_memory_space_constraint(v, pltpu.SMEM) for v in tables]
    hx = swap(ma, mb, "gx")
    hy = swap(ya, yb, "gy")
    ymsg = arr(count * planes, lanes)
    flow_hy = hy
    g = None
    new = sv
    for s in range(SUBSTEPS):
        moving = s > 0
        if moving:
            halo = hy
            new, ma, mb, ya, yb, c03, s03 = call(
                edge_body,
                [inv(v) for v in (g, *hx, *hy, node_type, u)] + tables + [inv(w), inv(fixed)],
                [VM] * 7 + smem + [VM] * 2,
                (state, xmsg, xmsg, ymsg, ymsg, react_out, react_out),
                [VM] * 7,
                [rates, odd, keep],
            )
            hx = swap(ma, mb, "gx")
            hy = swap(ya, yb, "gy")
        ins = ([inv(g)] if moving else []) + [inv(v) for v in (new, c03, s03, u)]
        ins += tables + [inv(w)]
        specs = [VM] * (5 if moving else 4) + smem + [VM]
        if moving:
            ins += [inv(v) for v in (*halo, node_type, fixed)]
        specs += [VM] * (len(ins) - len(specs))
        final = s == SUBSTEPS - 1
        shape = pltpu.HBM((7, count, planes, rows, lanes), F32)
        g, *result = call(
            functools.partial(rest_body, moving, final),
            ins,
            specs,
            (state, shape) if final else (state,),
            [VM, ANY] if final else [VM],
            [inside, inside, rates_in] + ([state, pltpu.SemaphoreType.DMA((32,))] if final else []),
            alias={1 if moving else 0: 0},
        )
        if not moving:
            face = arr(9, rows, lanes)
            sent = call(
                functools.partial(faces_body, count),
                [inv(v) for v in (post, *hy)],
                [VM] * 3,
                (face, face),
                [VM] * 2,
            )
            flow_hx = swap(*sent, "gx")
    new_populations = call(
        functools.partial(flow_end_body, count),
        [inv(v) for v in (post, *flow_hx, *flow_hy, node_type)],
        [VM] * 6,
        pltpu.HBM((27, planes, rows, lanes), F32),
        ANY,
        [flows, sems[0]],
    )
    new_species = call(
        end_body,
        [inv(v) for v in (g, *hx, *hy, node_type, fixed)] + [hbm(result[0])],
        [VM] * 7 + [ANY],
        shape,
        ANY,
        [state, pltpu.SemaphoreType.DMA((32,))],
        alias={7: 0},
    )
    return new_populations, new_species


def solution(mesh):
    flow = P(None, "gx", "gy", None)
    kinds = P(None, None, "gx", "gy", None)
    return jax.shard_map(
        per_device,
        mesh=mesh,
        in_specs=(flow, kinds, P("gx", "gy", None), P(), P(), P(), P()),
        out_specs=(flow, kinds),
        check_vma=False,
    )
```

```python
import functools

import jax
import jax.numpy as jnp
from jax import lax
from jax.experimental import pallas as pl
from jax.experimental.pallas import tpu as pltpu
from jax.sharding import PartitionSpec as P


SUBSTEPS = 3
CONC = 20
OMEGA = 1.6
SPEED = 0.05
F32 = jnp.float32
BF16 = jnp.bfloat16
VEL = [(a, b, c) for a in (-1, 0, 1) for b in (-1, 0, 1) for c in (-1, 0, 1)]
WT = [(8.0 / 27, 2.0 / 27, 1.0 / 54, 1.0 / 216)[abs(a) + abs(b) + abs(c)] for a, b, c in VEL]
UPX = [q for q in range(27) if VEL[q][0] > 0]
DNX = [q for q in range(27) if VEL[q][0] < 0]
UPY = [q for q in range(27) if VEL[q][1] > 0]
DNY = [q for q in range(27) if VEL[q][1] < 0]
MIB = 1 << 20
VMEM = pltpu.VMEM
VM = pl.BlockSpec(memory_space=pltpu.VMEM)
SM = pl.BlockSpec(memory_space=pltpu.SMEM)
ANY = pl.BlockSpec(memory_space=pl.ANY)


def inv(x):
    return pltpu.with_memory_space_constraint(x, pltpu.VMEM)


def hbm(x):
    return pltpu.with_memory_space_constraint(x, pltpu.HBM)


def pairs(size, near):
    if near:
        return [(i, i ^ 1) for i in range(size)]
    return [(i, (i + 1 if i % 2 else i - 1) % size) for i in range(size)]


def is_even(axis):
    return lax.rem(lax.axis_index(axis), 2) == 0


def pick(even, one, other):
    return jnp.where(even, one, other)


class Halo:
    def __init__(self, near, far, axis):
        self.near, self.far, self.even = near, far, is_even(axis)

    def up(self, *at):
        return pick(self.even, self.far[at], self.near[at])

    def down(self, *at):
        return pick(self.even, self.near[at], self.far[at])


def call(body, ins, specs, outs, out_specs, scratch=(), alias=None, mib=12, cost=2_000_000):
    return pl.pallas_call(
        body,
        out_shape=outs,
        in_specs=specs,
        out_specs=out_specs,
        scratch_shapes=list(scratch),
        input_output_aliases=alias or {},
        compiler_params=pltpu.CompilerParams(vmem_limit_bytes=mib * MIB),
        cost_estimate=pl.CostEstimate(flops=cost, bytes_accessed=cost, transcendentals=0),
    )(*ins)


def react(rx, kc, c_ref, s_ref, w_ref, rt_ref, odd_ref=None, start=0, stop=None):
    species, rows, lanes = c_ref.shape
    part = slice(start, stop or rows)
    tiles = (part.stop - part.start) // 8
    half = w_ref.shape[1] // 2
    even = tiles - tiles % 2
    for j in range(half // 8):
        rate = c_ref[rx[0, j], part, :] * (c_ref[rx[1, j], part, :] * kc[j])
        at = slice(8 * j, 8 * j + 8)
        for t in range(0, even, 2):
            both = jnp.concatenate([rate[8 * t : 8 * t + 8], rate[8 * t + 8 : 8 * t + 16]], axis=1)
            high = both.astype(BF16)
            low = (both - high.astype(F32)).astype(BF16)
            rt_ref[at, lanes * t : lanes * (t + 2)] = high
            rt_ref[half + 8 * j : half + 8 * j + 8, lanes * t : lanes * (t + 2)] = low
        if even < tiles:
            last = rate[8 * even :]
            rest = last - last.astype(BF16).astype(F32)
            odd_ref[at, :] = jnp.concatenate([last, rest], axis=1).astype(BF16)
    if even < tiles:
        total = jnp.dot(w_ref[:, :half], odd_ref[...], preferred_element_type=F32)
        total = total[:, :lanes] + total[:, lanes:]
        s_ref[:, start + 8 * even : start + 8 * tiles, :] = total.reshape(species, 8, lanes)
    if even:
        total = jnp.dot(w_ref[...], rt_ref[:, : lanes * even], preferred_element_type=F32)
        for t in range(even):
            s_ref[:, start + 8 * t : start + 8 * t + 8, :] = total[
                :, lanes * t : lanes * (t + 1)
            ].reshape(species, 8, lanes)


def moments(f):
    rho = f[0]
    for q in range(1, 27):
        rho = rho + f[q]
    parts = []
    for axis in range(3):
        plus = None
        for q in range(27):
            if VEL[q][axis] > 0:
                diff = f[q] - f[26 - q]
                plus = diff if plus is None else plus + diff
        parts.append(plus)
    scale = 1.0 / rho
    return rho, [p * scale for p in parts]


def cross(g, rk, c, s, ux, sign):
    a = rk * c
    return (1.0 - rk) * g + (0.125 * (a + s) + (0.5 * sign) * (a * ux))


def bands(species):
    return [(k, min(8, species - k)) for k in range(0, species, 8)]


def stoichiometry(rv, w):
    rows, width = w.shape
    half = width // 2
    species, total = rows // 8, half // 8

    def iota(shape, axis):
        return lax.broadcasted_iota(jnp.int32, shape, axis)

    def hot(test):
        return jnp.where(test, 1.0, 0.0)

    label = iota((species, total), 0)
    net = hot(rv[2:3, :] == label) - hot(rv[0:1, :] == label) - hot(rv[1:2, :] == label)
    tall = hot((iota((rows, species), 0) >> 3) == iota((rows, species), 1)).astype(BF16)
    wide = hot((iota((total, half), 1) >> 3) == iota((total, half), 0)).astype(BF16)
    part = jnp.dot(tall, net.astype(BF16), preferred_element_type=F32)
    full = jnp.dot(part.astype(BF16), wide, preferred_element_type=F32)
    same = (iota((rows, half), 0) & 7) == (iota((rows, half), 1) & 7)
    full = jnp.where(same, full, 0.0).astype(BF16)
    w[:, :half] = full
    w[:, half:] = full


def first_body(pop, spec, react_in, kc_in, rk_in, mix_in, pv, sv, w, ma, mb, c03, s03, fixed,
               rx, kc, rk, mix, rt, rv, psem, ssem, tsem):
    planes, rows, lanes = pop.shape[1:]
    species = spec.shape[1]
    ends = (0, planes - 1)
    small = [
        pltpu.make_async_copy(src, dst, tsem.at[n])
        for n, (src, dst) in enumerate(
            ((react_in, rv), (react_in, rx), (kc_in, kc), (rk_in, rk), (mix_in, mix))
        )
    ]
    order = ends + tuple(range(1, planes - 1))
    kinds = [pltpu.make_async_copy(spec.at[:, :, x], sv.at[:, :, x], ssem.at[x]) for x in order]
    flows = [pltpu.make_async_copy(pop.at[:, x], pv.at[:, x], psem.at[x]) for x in order]
    for copy in small + kinds[:2] + flows + kinds[2:]:
        copy.start()
    for copy in small:
        copy.wait()
    stoichiometry(rv, w)
    for k in range(species):
        for n, value in enumerate((rk[k], mix[0, k], mix[1, k])):
            fixed[n, k : k + 1, :] = jnp.full((1, lanes), value, F32)
    for side in range(2):
        for n, i in enumerate((0, 1, 3, 4)):
            fixed[3 + 4 * side + n] = inlet_weight(i, side) * fixed[1 + side]
    for n, x in enumerate(ends):
        kinds[n].wait()

        def conc(k, carry, n=n, x=x):
            total = sv[0, k, x]
            for i in range(1, 7):
                total = total + sv[i, k, x]
            c03[k, n * rows : (n + 1) * rows, :] = total
            return carry

        lax.fori_loop(0, species, conc, 0, unroll=CONC)
    react(rx, kc, c03, s03, w, rt)
    speeds = []
    for n, x in enumerate(ends):
        flows[n].wait()
        speeds.append(moments([pv[q, x] for q in range(27)])[1][0])
    send_faces(sv, rk, c03, s03, speeds, ma, mb)
    for copy in flows[2:] + kinds[2:]:
        copy.wait()


def second_body(pv, sv, c03, s03, rx, kc, w, fixed, u, post, ya, yb, edge_c, edge_s, odd, keep):
    species, planes, rows, lanes = sv.shape[1:]
    inner = range(1, planes - 1)
    for k in range(species):
        edge_c[k] = jnp.zeros(edge_c.shape[1:], F32)
    collide_flow(pv, u, post)
    flat = sv.reshape(7 * species * planes * rows, lanes)
    height = edge_c.shape[1]
    cflat = edge_c.reshape(species * height, lanes)
    for x in inner:
        for side, row in ((0, 0), (1, rows - 1)):
            for k, size in bands(species):
                values = [
                    flat[pl.ds(((i * species + k) * planes + x) * rows + row, size, planes * rows), :]
                    for i in range(7)
                ]
                total = values[0]
                for i in range(1, 7):
                    total = total + values[i]
                spot = k * height + 2 * (x - 1) + side
                cflat[pl.ds(spot, size, height), :] = total
                keep[side, x * species + k : x * species + k + size, :] = values[3 if side else 4]
    react(rx, kc, edge_c, edge_s, w, None, odd)
    send_rows(sv, keep, c03, s03, edge_c, edge_s, fixed, u, ya, yb)
    first, last, even = edge_flags()
    for n in range(9):
        for x in range(planes):
            at = slice((species + n) * planes + x, (species + n) * planes + x + 1)
            top = jnp.where(last, 0.0, post[UPY[n], x, rows - 1 : rows, :])
            bottom = jnp.where(first, 0.0, post[DNY[n], x, 0:1, :])
            ya[at, :] = pick(even, top, bottom)
            yb[at, :] = pick(even, bottom, top)


def edge_flags():
    rank, size = lax.axis_index("gy"), lax.axis_size("gy")
    return rank == 0, rank == size - 1, is_even("gy")


def send_rows(state, keep, c03, s03, edge_c, edge_s, fixed, u, ya, yb):
    species, planes, rows, lanes = state.shape[1:]
    fresh = state.reshape(7 * species * planes * rows, lanes)
    first, last, even = edge_flags()
    for x in range(planes):
        if x in (0, planes - 1):
            cref, sref, base = c03, s03, (x > 0) * rows
        else:
            cref, sref, base = edge_c, edge_s, 2 * (x - 1)
        height = cref.shape[1]
        cflat = cref.reshape(species * height, lanes)
        sflat = sref.reshape(species * height, lanes)
        for k, size in bands(species):
            halo = slice(x * species + k, x * species + k + size)
            sent = []
            for side, row, off in ((0, 0, first), (1, rows - 1, last)):
                i, sign = (3, 1.0) if side else (4, -1.0)
                if x in (0, planes - 1):
                    spot = base + row
                    at = ((i * species + k) * planes + x) * rows + row
                    value = fresh[pl.ds(at, size, planes * rows), :]
                else:
                    spot = base + side
                    value = keep[side, halo, :]
                c = cflat[pl.ds(k * height + spot, size, height), :]
                s = sflat[pl.ds(k * height + spot, size, height), :]
                uy = u[1, x, row : row + 1, :]
                value = cross(value, fixed[0, k : k + size, :], c, s, uy, sign)
                sent.append(jnp.where(off, 0.0, value))
            ya[halo, :] = pick(even, sent[1], sent[0])
            yb[halo, :] = pick(even, sent[0], sent[1])


def send_faces(state, rk, c03, s03, speeds, ma, mb):
    species, planes, rows = state.shape[1:4]
    even = is_even("gx")

    def send(k, carry):
        low = cross(state[2, k, 0], rk[k], c03[k, :rows, :], s03[k, :rows, :], speeds[0], -1.0)
        part = slice(rows, 2 * rows)
        high = cross(
            state[1, k, planes - 1], rk[k], c03[k, part, :], s03[k, part, :], speeds[1], 1.0
        )
        ma[k] = pick(even, high, low)
        mb[k] = pick(even, low, high)
        return carry

    lax.fori_loop(0, species, send, 0, unroll=5)


def relaxed(rho, v, q):
    still = 1.0 - 1.5 * (v[0] * v[0] + v[1] * v[1] + v[2] * v[2])
    along = None
    for axis in range(3):
        if VEL[q][axis]:
            term = v[axis] if VEL[q][axis] > 0 else -v[axis]
            along = term if along is None else along + term
    return still, OMEGA * rho, (still + 4.5 * along * along, 3.0 * along)


def collide_flow(pv, u, post):
    for x in range(pv.shape[1]):
        f = [pv[q, x] for q in range(27)]
        rho, v = moments(f)
        for axis in range(3):
            u[axis, x] = v[axis]
        for q in range(14, 27):
            still, scaled, (even, odd) = relaxed(rho, v, q)
            ws = WT[q] * scaled
            for p, value in ((q, even + odd), (26 - q, even - odd)):
                post[p, x] = (1.0 - OMEGA) * f[p] + ws * value
        post[13, x] = (1.0 - OMEGA) * f[13] + WT[13] * scaled * still


def row_index(rows, lanes):
    return lax.broadcasted_iota(jnp.int32, (rows, lanes), 0)


def gather(k, x, g, hx, hy, pairs):
    species, planes, rows, lanes = g.shape[1:]
    out = {}
    if 0 in pairs:
        out[0] = g[0, k, x]
    if 1 in pairs:
        out[1] = g[1, k, x - 1] if x > 0 else hx.up(k)
        out[2] = g[2, k, x + 1] if x < planes - 1 else hx.down(k)
    if 3 in pairs:
        flat = g.reshape(7 * species * planes * rows, lanes)
        at = row_index(8, lanes)
        spot = pl.ds(x * species + k, 1)
        for i, step, halo in ((3, -1, hy.up), (4, 1, hy.down)):
            base = ((i * species + k) * planes + x) * rows + step
            parts = [flat[pl.ds(base + t, 8), :] for t in range(0, rows, 8)]
            edge, row = (0, 0) if step < 0 else (-1, 7)
            parts[edge] = jnp.where(at == row, halo(spot, slice(None)), parts[edge])
            out[i] = jnp.concatenate(parts, axis=0)
    if 5 in pairs:
        out[5] = pltpu.roll(g[5, k, x], 1, 1)
        out[6] = pltpu.roll(g[6, k, x], lanes - 1, 1)
    return out


def masks(nt, x):
    rows = nt.shape[1]
    return nt[x] == 1, nt[x, :8, :] == 2, nt[x, rows - 8 :, :] == 3


def settle(value, kind, k, fixed, base):
    _, low, high = kind
    spot = pl.ds(k, 1)
    first = jnp.where(low, fixed[base[0], spot, :], value[:8])
    if value.shape[0] == 8:
        return jnp.where(high, fixed[base[1], spot, :], first)
    last = jnp.where(high, fixed[base[1], spot, :], value[-8:])
    return jnp.concatenate([first, value[8:-8], last] if value.shape[0] > 16 else [first, last], 0)


def walled(moved, kind, k, fixed):
    swap = (0, 2, 1, 4, 3, 6, 5)
    out = {}
    for i, m in moved.items():
        n = {0: 0, 3: 2, 4: 3}.get(i, 1)
        value = m if i == 0 else jnp.where(kind[0], moved[swap[i]], m)
        out[i] = settle(value, kind, k, fixed, (3 + n, 7 + n))
    return out


def inlet_weight(i, side):
    tilt = 4.0 * SPEED * (1.0 if side == 0 else -1.0)
    return {0: 0.25, 3: 0.125 * (1.0 + tilt), 4: 0.125 * (1.0 - tilt)}.get(i, 0.125)


def ready_body(g, hya, hyb, nt, rx, kc, w, fixed, new, c03, keep, edge_c, edge_s, odd):
    hy = Halo(hya, hyb, "gy")
    species, planes, rows, lanes = g.shape[1:]
    flat = g.reshape(7 * species * planes * rows, lanes)
    height = edge_c.shape[1]
    cflat = edge_c.reshape(species * height, lanes)
    for k in range(species):
        edge_c[k] = jnp.zeros((height, lanes), F32)
    for x in range(1, planes - 1):
        for side, row in ((0, 0), (1, rows - 1)):
            kind = nt[x, row : row + 1, :]
            for k, size in bands(species):

                def load(i, plane, r, k=k, size=size):
                    at = ((i * species + k) * planes + plane) * rows + r
                    return flat[pl.ds(at, size, planes * rows), :]

                halo = slice(x * species + k, x * species + k + size)
                moved = {
                    0: load(0, x, row),
                    1: load(1, x - 1, row),
                    2: load(2, x + 1, row),
                    3: hy.up(halo, slice(None)) if side == 0 else load(3, x, row - 1),
                    4: hy.down(halo, slice(None)) if side == 1 else load(4, x, row + 1),
                    5: pltpu.roll(load(5, x, row), 1, 1),
                    6: pltpu.roll(load(6, x, row), lanes - 1, 1),
                }
                wide = jnp.broadcast_to(kind, (size, lanes))
                inlet = wide == 2 + side
                value = fixed[1 + side, k : k + size, :]
                total = moved[0]
                for i in range(1, 7):
                    total = total + moved[i]
                total = jnp.where(inlet, value, total)
                i = 3 if side else 4
                kept = jnp.where(wide == 1, moved[7 - i], moved[i])
                kept = jnp.where(inlet, inlet_weight(i, side) * value, kept)
                spot = k * height + 2 * (x - 1) + side
                cflat[pl.ds(spot, size, height), :] = total
                keep[side, halo, :] = kept
    for n, x in enumerate((0, planes - 1)):
        kind = masks(nt, x)

        def step(k, carry, n=n, x=x, kind=kind):
            moved = gather(k, x, g, None, hy, (0, 3, 5))
            total = g[2, k, 1] if n == 0 else g[1, k, planes - 2]
            for m in moved.values():
                total = total + m
            for i, value in walled(moved, kind, k, fixed).items():
                new[i, k, x] = value
            c03[k, n * rows : (n + 1) * rows, :] = total
            return carry

        lax.fori_loop(0, species, step, 0, unroll=CONC)
    react(rx, kc, edge_c, edge_s, w, None, odd)


def edge_body(g, hxa, hxb, nt, u, rx, kc, rk, w, fixed, keep, edge_c, edge_s, new_in, part, new,
              c03, ma, mb, ya, yb, s03, rt):
    del new_in, part
    hx = Halo(hxa, hxb, "gx")
    species, planes, rows, _ = g.shape[1:]
    ends = (0, planes - 1)
    for n, x in enumerate(ends):
        kind = masks(nt, x)

        def step(k, carry, n=n, x=x, kind=kind):
            moved = gather(k, x, g, hx, None, (1,))
            part = slice(n * rows, (n + 1) * rows)
            total = c03[k, part, :] + moved[1 + n]
            for i, value in walled(moved, kind, k, fixed).items():
                new[i, k, x] = value
            c03[k, part, :] = settle(total, kind, k, fixed, (1, 2))
            return carry

        lax.fori_loop(0, species, step, 0, unroll=CONC)
    react(rx, kc, c03, s03, w, rt)
    send_faces(new, rk, c03, s03, [u[0, x] for x in ends], ma, mb)
    send_rows(new, keep, c03, s03, edge_c, edge_s, fixed, u, ya, yb)


def rest_body(moving, final, *refs):
    refs = list(refs)
    g = refs.pop(0) if moving else None
    start, c03, s03, u, rx, kc, rk, w = [refs.pop(0) for _ in range(8)]
    if moving:
        hya, hyb, nt, fixed = [refs.pop(0) for _ in range(4)]
        hy = Halo(hya, hyb, "gy")
    new = refs.pop(0)
    result = refs.pop(0) if final else None
    c12, s12, rt = refs[:3]
    species, planes, rows, _ = new.shape[1:]
    for x in range(1, planes - 1):
        kind = masks(nt, x) if moving else None

        def step(k, carry, x=x, kind=kind):
            if moving:
                moved = gather(k, x, g, None, hy, (0, 1, 3, 5))
                values = walled(moved, kind, k, fixed)
            else:
                moved = {i: start[i, k, x] for i in range(7)}
            total = moved[0]
            for i in range(1, 7):
                total = total + moved[i]
            if moving:
                for i in range(7):
                    new[i, k, x] = values[i]
                total = settle(total, kind, k, fixed, (1, 2))
            c12[k, (x - 1) * rows : x * rows, :] = total
            return carry

        lax.fori_loop(0, species, step, 0, unroll=CONC)
    react(rx, kc, c12, s12, w, rt)
    chunk = 5 if final and species % 5 == 0 else species
    copies = []
    for begin in range(0, species, chunk):
        end = begin + chunk
        for x in range(planes):
            ux, uy, uz = 0.5 * u[0, x], 0.5 * u[1, x], 0.5 * u[2, x]
            if x in (0, planes - 1):
                cr, sr, half = c03, s03, slice((x > 0) * rows, (x > 0) * rows + rows)
            else:
                cr, sr, half = c12, s12, slice((x - 1) * rows, x * rows)

            def collide(k, carry, x=x, cr=cr, sr=sr, half=half, ux=ux, uy=uy, uz=uz):
                r = rk[k]
                keep = 1.0 - r
                a = r * cr[k, half, :]
                base1 = 0.125 * (a + sr[k, half, :])
                new[0, k, x] = keep * new[0, k, x] + (base1 + base1)
                for i, v in ((1, ux), (3, uy), (5, uz)):
                    d = a * v
                    up = keep * new[i, k, x] + (base1 + d)
                    down = keep * new[i + 1, k, x] + (base1 - d)
                    new[i, k, x] = up
                    new[i + 1, k, x] = down
                return carry

            lax.fori_loop(begin, end, collide, 0, unroll=5)
        if final:
            copies += put_out(
                {0: range(planes), 5: range(planes), 1: range(1, planes - 1)},
                slice(begin, end), new, None, None, nt, fixed, result, refs[3], refs[4], len(copies),
            )
    for copy in copies:
        copy.wait()


def put_out(cover, part, g, hx, hy, nt, fixed, result, buf, sem, used):
    planes = g.shape[2]
    for x in range(planes):
        pairs = [p for p, xs in cover.items() if x in xs]
        kind = masks(nt, x)
        for k in range(part.start, part.stop):
            values = walled(gather(k, x, g, hx, hy, pairs), kind, k, fixed)
            for i, value in values.items():
                buf[i, k, x] = value
    copies = []
    for pair, xs in cover.items():
        for i in (0,) if pair == 0 else (pair, pair + 1):
            if len(xs) == planes or 0 not in xs:
                spans = [slice(xs[0], xs[-1] + 1)]
            else:
                spans = [slice(x, x + 1) for x in xs]
            for span in spans:
                at = (i, part, span)
                copies.append(
                    pltpu.make_async_copy(buf.at[at], result.at[at], sem.at[used + len(copies)])
                )
    for copy in copies:
        copy.start()
    return copies


def faces_body(species, post, hya, hyb, fa, fb):
    planes = post.shape[1]
    hy = Halo(hya, hyb, "gy")
    even = is_even("gx")
    for n in range(9):
        high = flow_moved(UPX[n], planes - 1, post, hy, species * planes)
        low = flow_moved(DNX[n], 0, post, hy, species * planes)
        fa[n] = pick(even, high, low)
        fb[n] = pick(even, low, high)


def flow_moved(q, src, post, hy, base):
    planes, rows, lanes = post.shape[1:]
    at = row_index(rows, lanes)
    step = VEL[q][1]
    value = post[q, src]
    if step:
        row, queue, halo = (0, UPY, hy.up) if step > 0 else (rows - 1, DNY, hy.down)
        spot = base + queue.index(q) * planes + src
        shifted = pltpu.roll(value, step % rows, 0)
        value = jnp.where(at == row, halo(slice(spot, spot + 1), slice(None)), shifted)
    return value


def flow_end_body(species, post, fxa, fxb, hya, hyb, nt, result, out, sem):
    planes, _, lanes = post.shape[1:]
    base = species * planes
    hx, hy = Halo(fxa, fxb, "gx"), Halo(hya, hyb, "gy")
    copies = []
    for x in list(range(1, planes - 1)) + [0, planes - 1]:
        kind = nt[x]
        wall = kind == 1
        inlet = kind >= 2
        fuel = kind == 2
        for q in range(13, 27):
            moved = {}
            for p in {q, 26 - q}:
                a, _, c = VEL[p]
                src = x - a
                if src < 0:
                    value = hx.up(UPX.index(p))
                elif src >= planes:
                    value = hx.down(DNX.index(p))
                else:
                    value = flow_moved(p, src, post, hy, base)
                if c:
                    value = pltpu.roll(value, 1 if c > 0 else lanes - 1, 1)
                moved[p] = value
            for p in moved:
                cu = VEL[p][1] * SPEED
                fixed = [
                    WT[p] * (1.0 + 3.0 * s * cu + 4.5 * cu * cu - 1.5 * SPEED * SPEED)
                    for s in (1.0, -1.0)
                ]
                value = moved[p] if p == 13 else jnp.where(wall, moved[26 - p], moved[p])
                out[p, x] = jnp.where(inlet, jnp.where(fuel, fixed[0], fixed[1]), value)
        copies.append(pltpu.make_async_copy(out.at[:, x], result.at[:, x], sem.at[x]))
        copies[-1].start()
    for copy in copies:
        copy.wait()


def end_body(g, hxa, hxb, hya, hyb, nt, fixed, before, out, buf, sem):
    del before
    species, planes = g.shape[1:3]
    hx, hy = Halo(hxa, hxb, "gx"), Halo(hya, hyb, "gy")
    chunk = 5 if species % 5 == 0 else species
    copies = []
    for begin in range(0, species, chunk):
        copies += put_out(
            {3: range(planes), 1: (0, planes - 1)},
            slice(begin, begin + chunk), g, hx, hy, nt, fixed, out, buf, sem, len(copies),
        )
    for copy in copies:
        copy.wait()


def per_device(populations, species, node_type, reactions, rate_const, species_rate, inlet_mix):
    planes, rows, lanes = node_type.shape
    count = species.shape[1]
    total = reactions.shape[0]
    pad = total % 2
    if pad:
        reactions = jnp.pad(reactions, ((0, pad), (0, 0)))
        rate_const = jnp.pad(rate_const, (0, pad))
        total += pad
    nt = inv(node_type)
    smem = [SM] * 3

    def arr(*shape):
        return VMEM(shape, F32)

    state = arr(7, count, planes, rows, lanes)
    inner = planes - 2
    edges = -(-2 * inner // 8) * 8
    edge_out = arr(count, edges, lanes)
    react_out = arr(count, 2 * rows, lanes)
    rates = VMEM((2 * total * 8, 2 * rows // 8 * lanes), BF16)
    odd = VMEM((total * 8, 2 * lanes), BF16)
    rates_in = VMEM((2 * total * 8, inner * rows // 8 * lanes), BF16)
    inside = VMEM((count, inner * rows, lanes), F32)

    def swap(near, far, axis):
        size = lax.axis_size(axis)
        far = lax.ppermute(far, axis, pairs(size, False))
        near = lax.ppermute(near, axis, pairs(size, True))
        return near, far

    xmsg = arr(count, rows, lanes)
    sems = [pltpu.SemaphoreType.DMA((planes,)), pltpu.SemaphoreType.DMA((planes,))]
    ints = pltpu.SMEM((3, total), jnp.int32)
    flows = arr(27, planes, rows, lanes)
    ymsg = arr((count + 9) * planes, lanes)
    keep = arr(2, count * planes, lanes)
    pv, sv, w, ma, mb, c03, s03, fixed, *tables = call(
        first_body,
        [hbm(v) for v in (populations, species, reactions.T, rate_const, species_rate, inlet_mix)],
        [ANY] * 6,
        (flows, state, VMEM((count * 8, 2 * total * 8), BF16), xmsg, xmsg, react_out, react_out,
         arr(11, count, lanes), ints, pltpu.SMEM((total,), F32), pltpu.SMEM((count,), F32)),
        [VM] * 8 + [SM] * 3,
        [pltpu.SMEM((2, count), F32), rates, VMEM((3, total), jnp.int32)] + sems
        + [pltpu.SemaphoreType.DMA((5,))],
    )
    tables = [pltpu.with_memory_space_constraint(v, pltpu.SMEM) for v in tables]
    hx = swap(ma, mb, "gx")
    u, post, ya, yb = call(
        second_body,
        [inv(v) for v in (pv, sv, c03, s03)] + tables[:2] + [inv(w), inv(fixed)],
        [VM] * 4 + [SM] * 2 + [VM] * 2,
        (arr(3, planes, rows, lanes), flows, ymsg, ymsg),
        [VM] * 4,
        [edge_out, edge_out, odd, keep],
    )
    hy = swap(ya, yb, "gy")
    ymsg = arr(count * planes, lanes)
    flow_hy = hy
    g = None
    new = sv
    for s in range(SUBSTEPS):
        moving = s > 0
        if moving:
            halo = hy
            new, c03, kept, edge_c, edge_s = call(
                ready_body,
                [inv(v) for v in (g, *hy, node_type)] + tables[:2] + [inv(w), inv(fixed)],
                [VM] * 4 + [SM] * 2 + [VM] * 2,
                (state, react_out, keep, edge_out, edge_out),
                [VM] * 5,
                [odd],
            )
            new, c03, ma, mb, ya, yb, s03 = call(
                edge_body,
                [inv(v) for v in (g, *hx, node_type, u)] + tables
                + [inv(v) for v in (w, fixed, kept, edge_c, edge_s, new, c03)],
                [VM] * 5 + smem + [VM] * 7,
                (state, react_out, xmsg, xmsg, ymsg, ymsg, react_out),
                [VM] * 7,
                [rates],
                alias={13: 0, 14: 1},
            )
            hx = swap(ma, mb, "gx")
            hy = swap(ya, yb, "gy")
        ins = ([inv(g)] if moving else []) + [inv(v) for v in (new, c03, s03, u)]
        ins += tables + [inv(w)]
        specs = [VM] * (5 if moving else 4) + smem + [VM]
        if moving:
            ins += [inv(v) for v in (*halo, node_type, fixed)]
        specs += [VM] * (len(ins) - len(specs))
        final = s == SUBSTEPS - 1
        shape = pltpu.HBM((7, count, planes, rows, lanes), F32)
        g, *result = call(
            functools.partial(rest_body, moving, final),
            ins,
            specs,
            (state, shape) if final else (state,),
            [VM, ANY] if final else [VM],
            [inside, inside, rates_in] + ([state, pltpu.SemaphoreType.DMA((32,))] if final else []),
            alias={1 if moving else 0: 0},
        )
        if not moving:
            face = arr(9, rows, lanes)
            sent = call(
                functools.partial(faces_body, count),
                [inv(v) for v in (post, *hy)],
                [VM] * 3,
                (face, face),
                [VM] * 2,
            )
            flow_hx = swap(*sent, "gx")
    new_populations = call(
        functools.partial(flow_end_body, count),
        [inv(v) for v in (post, *flow_hx, *flow_hy, node_type)],
        [VM] * 6,
        pltpu.HBM((27, planes, rows, lanes), F32),
        ANY,
        [flows, sems[0]],
    )
    new_species = call(
        end_body,
        [inv(v) for v in (g, *hx, *hy, node_type, fixed)] + [hbm(result[0])],
        [VM] * 7 + [ANY],
        shape,
        ANY,
        [state, pltpu.SemaphoreType.DMA((32,))],
        alias={7: 0},
    )
    return new_populations, new_species


def solution(mesh):
    flow = P(None, "gx", "gy", None)
    kinds = P(None, None, "gx", "gy", None)
    return jax.shard_map(
        per_device,
        mesh=mesh,
        in_specs=(flow, kinds, P("gx", "gy", None), P(), P(), P(), P()),
        out_specs=(flow, kinds),
        check_vma=False,
    )
```
